32 devices in a mesh: mesh: 8 (over z, y), mode: 4 (over x, core).
Axes of the slice: x: 2, y: 2, z: 4, core: 2. Of those that a mesh axis runs over, the one named last changes fastest.
Arguments:
- field: float32 [256, 131072], P('mode', 'mesh'), may hold values from -6 to 6
- right_side: float32 [256, 131072], P('mode', 'mesh'), may hold values from -6 to 6
- coefficient: float32 [2, 131072], P(None, 'mesh'), may hold values from 0.3 to 3
- precond: float32 [131072], P('mesh'), may hold values from 0.1 to 1
- blocks: bfloat16 [2, 7, 256, 256], replicated, may hold values from -0.125 to 0.125
- couplings: int32 [512, 7], P('mesh'), may hold values from 0 to 1, as said below
- chaos_values: bfloat16 [48, 16, 16], replicated, may hold values from -0.875 to 0.875
- chaos_index: int32 [48, 2], replicated, may hold values from 0 to 15, as said below
Outputs:
- updated: float32 [256, 131072], P('mode', 'mesh')
- residual: float32 [256, 131072], P('mode', 'mesh')
The draws below stay inside these ranges and needn't reach their ends.
Inputs may be any that keep to these rules, and one draw needn't show every extreme that they name: couplings[i, c] links block i to block i + c - 3; it is 1 for c = 3 and wherever block i + c - 3 lies in another slab of 16384 unknowns. `chaos_index`: rows 3 r to 3 r + 2 hold row block r, with column blocks r and two other distinct blocks.
All inputs are finite; a program needn't handle non-finite values.
Results may differ from the reference program's by a relative error of at most 0.0032.
Values may be sent and summed in bfloat16 or wider, within the bound.
A program may use at most 128 MiB of HBM per device.

```python
import math
import jax
import jax.numpy as jnp

P_SIZE = 256
PBLK = 16
B = 256
S_DEV = 16384
PB = 16
NNZB = 48
N = 131072
NBLK = 512


def draw_couplings(key, part):
    coin_flip = jax.random.randint(key, (NBLK, 7), 0, 4)
    kept_links = (coin_flip > 0).astype(jnp.int32)
    in_slab = jnp.arange(NBLK, dtype=jnp.int32) % (S_DEV // B)
    offsets = jnp.arange(7, dtype=jnp.int32)
    target = in_slab[:, None] + offsets[None, :] - 3
    forced = (target < 0) | (target >= S_DEV // B) | (offsets[None, :] == 3)
    return jnp.where(forced, 1, kept_links).astype(jnp.int32)


def pick_shifts(row_key):
    return jax.random.permutation(row_key, PBLK - 1)[:2].astype(jnp.int32) + 1


def draw_chaos_index(key, part):
    row_keys = jax.random.split(jax.random.fold_in(key, 7), PBLK)
    shifts = jax.vmap(pick_shifts)(row_keys)
    row_ids = jnp.arange(PBLK, dtype=jnp.int32)
    columns = jnp.stack([row_ids, (row_ids + shifts[:, 0]) % PBLK, (row_ids + shifts[:, 1]) % PBLK], axis=1)
    repeated = jnp.broadcast_to(row_ids[:, None], (PBLK, 3))
    return jnp.stack([repeated, columns], axis=2).reshape(NNZB, 2).astype(jnp.int32)


def level_of(rng, dims, shards, smallest, high):
    def one(axis_at, blocks):
        heights = jax.random.uniform(jax.random.fold_in(jax.random.fold_in(rng, 6), axis_at), (blocks,), jnp.float32, smallest / len(shards), high / len(shards))
        return jnp.repeat(jnp.exp(heights), dims[axis_at] // blocks).reshape((-1,) + (1,) * (len(dims) - axis_at - 1))

    factor_of = one(*shards[0])
    for cut in shards[1:]:
        factor_of = factor_of * one(*cut)
    return factor_of


def noise(stream_key, shape, scale, limit, pieces=(), held_as=jnp.bfloat16):
    entries = scale * jax.random.normal(stream_key, shape, jnp.float32)
    if pieces:
        entries = entries * level_of(stream_key, shape, pieces, -0.22, 0.18)
    return jnp.clip(entries, -limit, limit).astype(held_as)


def setup_inputs(seed: int = 0) -> dict:
    key_list = jax.random.split(jax.random.key(seed), 9)
    field = noise(key_list[0], (P_SIZE, N), 1.0, 6.0, ((0, 4), (1, 8)), jnp.float32)
    right_side = noise(key_list[1], (P_SIZE, N), 1.0, 6.0, ((0, 4), (1, 8)), jnp.float32)
    coefficient = jnp.clip(jnp.exp(math.log(3.0) - 2.3025851 * jax.random.uniform(key_list[2], (2, N), jnp.float32) ** level_of(key_list[2], (2, N), ((1, 8),), -0.2, 0.2)), 0.3, 3.0)
    precond = jnp.clip(jnp.exp(math.log(1.0) - 2.3025851 * jax.random.uniform(key_list[3], (N,), jnp.float32) ** level_of(key_list[3], (N,), ((0, 8),), -0.2, 0.2)), 0.1, 1.0)
    blocks = noise(key_list[4], (2, 7, B, B), (7 * B) ** -0.5, 0.125)
    couplings = draw_couplings(jax.random.fold_in(key_list[8], 71), 0)
    chaos_values = noise(key_list[6], (NNZB, PB, PB), (3 * PB) ** -0.5, 0.875)
    chaos_index = draw_chaos_index(jax.random.fold_in(key_list[8], 71), 0)
    return {"field": field, "right_side": right_side, "coefficient": coefficient, "precond": precond, "blocks": blocks, "couplings": couplings, "chaos_values": chaos_values, "chaos_index": chaos_index}


def stiffness(lowered, blocks, couplings, coefficient, which_term):
    mode_count = lowered.shape[0]
    block_count = lowered.shape[1] // B
    padded = jnp.pad(lowered, ((0, 0), (3 * B, 3 * B)))
    summed = jnp.zeros((mode_count, block_count, B), jnp.float32)
    for offset in range(7):
        window = padded[:, offset * B: offset * B + block_count * B].reshape(mode_count * block_count, B)
        product = jnp.dot(window, blocks[which_term, offset], preferred_element_type=jnp.float32)
        product = product.reshape(mode_count, block_count, B)
        summed = summed + product * couplings[:, offset].astype(jnp.float32)[None, :, None]
    return summed.reshape(mode_count, -1) * coefficient[which_term][None, :]


def chaos_matrix(chaos_values, chaos_index):
    block_ids = jnp.arange(PBLK, dtype=jnp.int32)
    row_hits = (chaos_index[:, 0:1] == block_ids[None, :]).astype(jnp.float32)
    col_hits = (chaos_index[:, 1:2] == block_ids[None, :]).astype(jnp.float32)
    spread_blocks = jnp.einsum("br,bc,bij->ricj", row_hits, col_hits, chaos_values.astype(jnp.float32))
    return spread_blocks.reshape(P_SIZE, P_SIZE).astype(jnp.bfloat16)


def reference(field, right_side, coefficient, precond, blocks, couplings, chaos_values, chaos_index):
    lowered = field.astype(jnp.bfloat16)
    diffused = stiffness(lowered, blocks, couplings, coefficient, 0)
    spread = stiffness(lowered, blocks, couplings, coefficient, 1).astype(jnp.bfloat16)
    matrix = chaos_matrix(chaos_values, chaos_index)
    mixed = jnp.dot(matrix, spread, preferred_element_type=jnp.float32)
    residual = right_side - (diffused + mixed)
    updated = field + precond[None, :] * residual
    return updated, residual
```

```python
import functools

import jax
import jax.numpy as jnp
from jax import lax
from jax.experimental import pallas as pl
from jax.experimental.pallas import tpu as pltpu
from jax.sharding import PartitionSpec as P

MESH = pl.DeviceIdType.MESH
REACH = 3


def kernel(
    modes, slabs, group,
    field, right, coefficient, blocks, couplings, chaos_values, chaos_index,
    fbuf, rbuf,
    low, weights, coef, gathered, matrix, hits,
    field_sem, right_sem, weight_sem, coef_sem,
    halo_send, halo_recv, near_send, far_send, forward_send, recv,
):
    rows, width = field.shape
    size = blocks.shape[-1]
    count = width // size
    groups = count // group
    span = group * size
    taps = 2 * REACH + 1
    pairs = modes // 2
    me = lax.axis_index("mode")
    slab = lax.axis_index("mesh")
    sibling = me + 1 - 2 * lax.rem(me, 2)
    peers = [lax.rem(me + 2 * j, modes) for j in range(1, pairs)]
    has_left = slab > 0
    has_right = slab < slabs - 1

    def columns(g):
        return pl.ds(pl.multiple_of(g * span, span), span)

    def field_copy(g):
        return pltpu.make_async_copy(field.at[:, columns(g)], fbuf.at[:, columns(g)], field_sem.at[g])

    def right_copy(g):
        return pltpu.make_async_copy(right.at[:, columns(g)], rbuf.at[:, columns(g)], right_sem.at[g])

    def weight_copy(k):
        return pltpu.make_async_copy(blocks.at[k], weights.at[k], weight_sem.at[k])

    field_copy(0).start()
    field_copy(groups - 1).start()
    weight_copy(1).start()
    coef_copy = pltpu.make_async_copy(coefficient, coef, coef_sem)
    coef_copy.start()

    @pl.loop(1, groups - 1)
    def _(g):
        field_copy(g).start()

    weight_copy(0).start()

    @pl.loop(0, groups)
    def _(g):
        right_copy(g).start()

    barrier = pltpu.get_barrier_semaphore()
    for other in [sibling] + peers:
        pl.semaphore_signal(barrier, inc=1, device_id={"mode": other}, device_id_type=MESH)

    @pl.when(has_left)
    def _():
        pl.semaphore_signal(barrier, inc=1, device_id={"mesh": slab - 1}, device_id_type=MESH)

    @pl.when(has_right)
    def _():
        pl.semaphore_signal(barrier, inc=1, device_id={"mesh": slab + 1}, device_id_type=MESH)

    def lower(g):
        for b in range(group):
            at = g * group + b
            cols = pl.ds(pl.multiple_of(at * size, size), size)
            low[REACH + at] = fbuf[:, cols].astype(jnp.bfloat16)

    field_copy(0).wait()
    lower(0)
    field_copy(groups - 1).wait()
    lower(groups - 1)

    pl.semaphore_wait(barrier, pairs + jnp.minimum(slab, 1) + jnp.minimum(slabs - 1 - slab, 1))

    to_left = pltpu.make_async_remote_copy(
        src_ref=low.at[pl.ds(REACH, REACH)], dst_ref=low.at[pl.ds(REACH + count, REACH)],
        send_sem=halo_send.at[0], recv_sem=halo_recv.at[0],
        device_id={"mesh": slab - 1}, device_id_type=MESH)
    to_right = pltpu.make_async_remote_copy(
        src_ref=low.at[pl.ds(count, REACH)], dst_ref=low.at[pl.ds(0, REACH)],
        send_sem=halo_send.at[1], recv_sem=halo_recv.at[1],
        device_id={"mesh": slab + 1}, device_id_type=MESH)

    @pl.when(has_left)
    def _():
        to_left.start()

    @pl.when(has_right)
    def _():
        to_right.start()

    @pl.when(jnp.logical_not(has_left))
    def _():
        low[pl.ds(0, REACH)] = jnp.zeros((REACH, rows, size), jnp.bfloat16)

    @pl.when(jnp.logical_not(has_right))
    def _():
        low[pl.ds(REACH + count, REACH)] = jnp.zeros((REACH, rows, size), jnp.bfloat16)

    field_copy(1).wait()
    lower(1)
    weight_copy(1).wait()
    coef_copy.wait()

    def stencil(g, k):
        tall = []
        for b in range(group):
            at = g * group + b
            wide = []
            for c in range(taps):
                keep = jnp.full((rows, size), couplings[c, at].astype(jnp.float32)).astype(jnp.bfloat16)
                wide.append(low[at + c] * keep)
            tall.append(jnp.concatenate(wide, axis=1))
        stacked = jnp.concatenate(tall, axis=0)
        return jnp.dot(stacked, weights[k].reshape(taps * size, size), preferred_element_type=jnp.float32)

    def piece(slot, g):
        return gathered.at[slot, pl.ds(g * group, group)]

    def send(slot, g, target, sem):
        return pltpu.make_async_remote_copy(
            src_ref=piece(slot, g), dst_ref=piece(slot, g), send_sem=sem, recv_sem=recv.at[slot, g],
            device_id={"mode": target}, device_id_type=MESH)

    def turn(t):
        return lax.rem(t + 1, groups)

    @pl.loop(0, groups)
    def _(t):
        g = turn(t)

        @pl.when(t + 2 <= groups - 2)
        def _():
            field_copy(t + 2).wait()
            lower(t + 2)

        @pl.when(jnp.logical_and(t == groups - 2, has_right))
        def _():
            to_left.wait_recv()

        @pl.when(jnp.logical_and(t == groups - 1, has_left))
        def _():
            to_right.wait_recv()

        sums = stencil(g, 1)
        for b in range(group):
            at = g * group + b
            cols = pl.ds(pl.multiple_of(at * size, size), size)
            scaled = sums[b * rows:(b + 1) * rows] * coef[1:2, cols]
            gathered[me, at] = scaled.astype(jnp.bfloat16)
        for j, peer in enumerate(peers):
            send(me, g, peer, far_send.at[j, g]).start()
        send(me, g, sibling, near_send.at[g]).start()

    part, _, links = chaos_values.shape
    total_rows = modes * rows
    per_row = links * part // total_rows
    column_of = lax.broadcasted_iota(jnp.int32, (1, total_rows), 1) // part
    for n in range(links):
        hits[n:n + 1, :] = (column_of == chaos_index[1, n]).astype(jnp.float32)
    lane_of = lax.broadcasted_iota(jnp.int32, (part, total_rows), 1)
    step_of = lax.broadcasted_iota(jnp.int32, (part, total_rows), 0)
    repeat = (lax.rem(lane_of, part) == step_of).astype(jnp.float32).astype(jnp.bfloat16)
    row_of = lax.broadcasted_iota(jnp.int32, (rows, links), 0)
    owner_of = lax.broadcasted_iota(jnp.int32, (rows, links), 1) // per_row
    owned = owner_of == row_of // part + me * (rows // part)
    built = jnp.zeros((rows, total_rows), jnp.float32)
    for i in range(part):
        spread_out = lax.dot_general(
            chaos_values[i], repeat, (((0,), (0,)), ((), ())), preferred_element_type=jnp.float32)
        placed = (spread_out * hits[0:links, :]).astype(jnp.bfloat16)
        mine = jnp.logical_and(owned, lax.rem(row_of, part) == i).astype(jnp.float32).astype(jnp.bfloat16)
        built = built + jnp.dot(mine, placed, preferred_element_type=jnp.float32)
    matrix[...] = built.astype(jnp.bfloat16)

    weight_copy(0).wait()

    @pl.loop(0, groups)
    def _(t):
        g = turn(t)
        right_copy(g).wait()
        sums = stencil(g, 0)
        for b in range(group):
            at = g * group + b
            cols = pl.ds(pl.multiple_of(at * size, size), size)
            rbuf[:, cols] = rbuf[:, cols] - sums[b * rows:(b + 1) * rows] * coef[0:1, cols]

    def mix(g):
        send(sibling, g, sibling, near_send.at[g]).wait_recv()
        for j, peer in enumerate(peers):
            other = peer + 1 - 2 * lax.rem(peer, 2)
            send(other, g, sibling, forward_send.at[j, g]).wait_recv()
        for b in range(group):
            at = g * group + b
            cols = pl.ds(pl.multiple_of(at * size, size), size)
            mixed = jnp.dot(
                matrix[...], gathered[:, at].reshape(modes * rows, size), preferred_element_type=jnp.float32)
            rbuf[:, cols] = rbuf[:, cols] - mixed

    def forward(g):
        for j, peer in enumerate(peers):
            send(peer, g, peer, far_send.at[j, g]).wait_recv()
            send(peer, g, sibling, forward_send.at[j, g]).start()

    forward(turn(0))

    @pl.loop(1, groups)
    def _(t):
        forward(turn(t))
        mix(turn(t - 1))

    mix(turn(groups - 1))

    @pl.loop(0, groups)
    def _(g):
        send(me, g, sibling, near_send.at[g]).wait_send()
        for j, peer in enumerate(peers):
            send(me, g, peer, far_send.at[j, g]).wait_send()
            send(peer, g, sibling, forward_send.at[j, g]).wait_send()

    @pl.when(has_left)
    def _():
        to_left.wait_send()

    @pl.when(has_right)
    def _():
        to_right.wait_send()


def masked_stencil(low, base, couplings, at, group, weights, taps, size):
    rows = low.shape[1]
    tall = []
    for b in range(group):
        wide = []
        for c in range(taps):
            keep = jnp.full((rows, size), couplings[c, at + b].astype(jnp.float32)).astype(jnp.bfloat16)
            wide.append(low[base + b + c] * keep)
        tall.append(jnp.concatenate(wide, axis=1))
    stacked = jnp.concatenate(tall, axis=0)
    return jnp.dot(stacked, weights.reshape(taps * size, size), preferred_element_type=jnp.float32)


def cheapest_cover(held, adjacent):
    chosen = lax.broadcasted_iota(jnp.int32, (8, 128), 0) * 128 + lax.broadcasted_iota(jnp.int32, (8, 128), 1)
    rest = chosen ^ (2 ** held - 1)
    columns = sum((chosen >> i) & 1 for i in range(held))
    uncovered = sum(jnp.where((rest & links) != 0, 1, 0) for links in adjacent)
    key = ((columns + uncovered) << (held + 4)) + (uncovered << held) + chosen
    key = jnp.where(chosen < 2 ** held, key.astype(jnp.float32), float(2 ** 23))
    return jnp.min(key).astype(jnp.int32)


def slots_of(held, chosen, adjacent):
    used = jnp.int32(0)
    columns = []
    for c in range(held):
        taken = (chosen >> c) & 1
        columns.append(jnp.where(taken == 1, used, -1))
        used = used + taken
    rows = []
    for links in adjacent:
        taken = jnp.where((links & ~chosen) != 0, 1, 0)
        rows.append(jnp.where(taken == 1, used, -1))
        used = used + taken
    return columns, rows


def along(shape, axis, shift, values):
    block = lax.broadcasted_iota(jnp.int32, shape, axis) >> shift
    found = jnp.full(shape, -1, jnp.int32)
    for i, value in enumerate(values):
        found = jnp.where(block == i, value, found)
    return found


def choose_kernel(
    group, fewest,
    field, coefficient, precond, blocks, chaos_values, chaos_index, index_row,
    choice, slots, weights, first, coef, scale, placed,
    values, wide_index, links_smem, sems,
):
    size = blocks.shape[-1]
    part, _, entries = chaos_values.shape
    total = placed.shape[1]
    held = total // part // 2
    shift = held.bit_length() - 1
    per_row = entries // (2 * held)
    near_span = pl.ds((group - REACH) * size, (group + 2 * REACH) * size)
    copies = [
        pltpu.make_async_copy(chaos_index, links_smem, sems.at[0]),
        pltpu.make_async_copy(index_row, wide_index, sems.at[1]),
        pltpu.make_async_copy(chaos_values, values, sems.at[2]),
        pltpu.make_async_copy(blocks.at[1], weights, sems.at[3]),
        pltpu.make_async_copy(field.at[:, near_span], first, sems.at[4]),
        pltpu.make_async_copy(coefficient, coef, sems.at[5]),
        pltpu.make_async_copy(precond, scale, sems.at[6]),
    ]
    for copy in copies:
        copy.start()

    copies[0].wait()
    adjacent = [[], []]
    for row in range(2 * held):
        side = row // held
        links = jnp.int32(0)
        for n in range(row * per_row, row * per_row + per_row):
            column = links_smem[1, n]
            links = links | (((column >> shift) ^ side) << (column & (held - 1)))
        adjacent[side].append(links)
    best = [cheapest_cover(held, links) for links in adjacent]
    needed = jnp.maximum(best[0] >> (held + 4), best[1] >> (held + 4))
    choice[0, 0] = jnp.maximum(needed - fewest, 0)
    for side in range(2):
        columns, rows = slots_of(held, best[side] & (2 ** held - 1), adjacent[side])
        for i, value in enumerate(columns + rows):
            slots[0, side * 2 * held + i] = value

    copies[1].wait()
    copies[2].wait()
    square = (entries, entries)
    wide_row = jnp.broadcast_to(wide_index[1:2, :], square).astype(jnp.float32)
    eye = lax.broadcasted_iota(jnp.int32, square, 0) == lax.broadcasted_iota(jnp.int32, square, 1)
    column_of = jnp.sum(jnp.where(eye, wide_row, 0.0), axis=1, keepdims=True)
    step = part.bit_length() - 1
    lane_block = (lax.broadcasted_iota(jnp.int32, (entries, total), 1) >> step).astype(jnp.float32)
    hits = (lane_block == column_of).astype(jnp.float32)
    lane_of = lax.broadcasted_iota(jnp.int32, (part, total), 1)
    step_of = lax.broadcasted_iota(jnp.int32, (part, total), 0)
    repeat = ((lane_of & (part - 1)) == step_of).astype(jnp.float32).astype(jnp.bfloat16)
    for i in range(part):
        spread_out = lax.dot_general(
            values[i], repeat, (((0,), (0,)), ((), ())), preferred_element_type=jnp.float32)
        placed[i * entries:(i + 1) * entries] = (spread_out * hits).astype(jnp.bfloat16)

    for copy in copies[3:]:
        copy.wait()


def packed_kernel(
    modes, slabs, group, entries, packed,
    field, right, blocks, couplings, slots, early, first, coef, scale, placed,
    fbuf, rbuf,
    low, later, gathered, outgoing, arrived, picks, matrix, links, slot_of,
    load_sem, field_sem, halo_send, halo_recv,
    near_send, near_recv, far_send, far_recv, forward_send, forward_recv,
):
    rows, width = field.shape
    size = blocks.shape[-1]
    count = width // size
    groups = count // group
    span = group * size
    taps = 2 * REACH + 1
    pairs = modes // 2
    both = 2 * rows
    total = 2 * both
    part = picks.shape[0] // packed
    held = both // part
    shift = part.bit_length() - 1
    per_row = entries // (2 * held)
    tall = packed * part
    me = lax.axis_index("mode")
    slab = lax.axis_index("mesh")
    sibling = me + 1 - 2 * lax.rem(me, 2)
    peer = lax.rem(me + 2, modes)
    core = lax.rem(me, 2)
    here = me // 2
    share = group // 2
    batch = groups // 4
    has_left = slab > 0
    has_right = slab < slabs - 1

    barrier = pltpu.get_barrier_semaphore()
    for other in [sibling, peer]:
        pl.semaphore_signal(barrier, inc=1, device_id={"mode": other}, device_id_type=MESH)

    @pl.when(has_left)
    def _():
        pl.semaphore_signal(barrier, inc=1, device_id={"mesh": slab - 1}, device_id_type=MESH)

    @pl.when(has_right)
    def _():
        pl.semaphore_signal(barrier, inc=1, device_id={"mesh": slab + 1}, device_id_type=MESH)

    def field_copy(q):
        cols = pl.ds(pl.multiple_of(q * batch * span, span), batch * span)
        return pltpu.make_async_copy(field.at[:, cols], fbuf.at[:, cols], field_sem.at[q])

    links_copy = pltpu.make_async_copy(couplings, links, load_sem.at[0])
    slots_copy = pltpu.make_async_copy(slots, slot_of, load_sem.at[1])
    later_copy = pltpu.make_async_copy(blocks.at[0], later, load_sem.at[2])
    right_copy = pltpu.make_async_copy(right, rbuf, load_sem.at[3])
    links_copy.start()
    slots_copy.start()
    for q in (0, 3, 1, 2):
        field_copy(q).start()
    later_copy.start()
    right_copy.start()

    def lower_block(at):
        cols = pl.ds(pl.multiple_of(at * size, size), size)
        low[REACH + at] = fbuf[:, cols].astype(jnp.bfloat16)

    def lower(g):
        for b in range(group):
            lower_block(g * group + b)

    def near(g):
        ours = gathered.at[core, pl.ds(g * group, group)]
        return pltpu.make_async_remote_copy(
            src_ref=ours, dst_ref=ours, send_sem=near_send, recv_sem=near_recv.at[g],
            device_id={"mode": sibling}, device_id_type=MESH)

    def far(g):
        return pltpu.make_async_remote_copy(
            src_ref=outgoing.at[pl.ds(g * share, share)],
            dst_ref=arrived.at[pl.ds(g * group + core * share, share)],
            send_sem=far_send, recv_sem=far_recv.at[g],
            device_id={"mode": peer}, device_id_type=MESH)

    def relay(g):
        ours = arrived.at[pl.ds(g * group + core * share, share)]
        return pltpu.make_async_remote_copy(
            src_ref=ours, dst_ref=ours, send_sem=forward_send, recv_sem=forward_recv.at[g],
            device_id={"mode": sibling}, device_id_type=MESH)

    def pack(g):
        near(g).wait_recv()
        for b in range(share):
            at = g * group + core * share + b
            outgoing[g * share + b] = jnp.dot(
                picks[...], gathered[:, at].reshape(both, size),
                preferred_element_type=jnp.float32).astype(jnp.bfloat16)
        far(g).start()

    def turn(t):
        return lax.rem(t + 1, groups)

    def stencil(g, weights):
        return masked_stencil(low, g * group, links, g * group, group, weights[...], taps, size)

    def spread(g):
        sums = stencil(g, early)
        for b in range(group):
            at = g * group + b
            cols = pl.ds(pl.multiple_of(at * size, size), size)
            scaled = sums[b * rows:(b + 1) * rows] * coef[1:2, cols]
            gathered[core, at] = scaled.astype(jnp.bfloat16)

    for b in range(group + 2 * REACH):
        low[group + b] = first[:, b * size:(b + 1) * size].astype(jnp.bfloat16)
    links_copy.wait()
    spread(1)
    pl.semaphore_wait(barrier, pairs + jnp.minimum(slab, 1) + jnp.minimum(slabs - 1 - slab, 1))
    near(1).start()

    slots_copy.wait()
    lane = lax.broadcasted_iota(jnp.int32, (1, part * entries), 1)
    lane_step = lax.div(lane, entries)
    lane_key = lane_step * 2 * held + lax.div(lane - lane_step * entries, per_row)

    def matrix_rows(height, start):
        row = lax.broadcasted_iota(jnp.int32, (height, 1), 0)
        row_key = (row & (part - 1)) * 2 * held + (row >> shift) + start
        wanted = (row_key == lane_key).astype(jnp.float32).astype(jnp.bfloat16)
        return jnp.dot(wanted, placed[...], preferred_element_type=jnp.float32)

    def half(values, side):
        return jnp.where(side == 0, values[:, 0:both], values[:, both:total])

    def slots_to(side, kind):
        first_slot = [slot_of[0, kind * held + i] for i in range(held)]
        other_slot = [slot_of[0, (2 + kind) * held + i] for i in range(held)]
        return [jnp.where(side == 0, a, b) for a, b in zip(first_slot, other_slot)]

    def chosen_rows(height, values):
        row = lax.broadcasted_iota(jnp.int32, (height, both), 0)
        column = lax.broadcasted_iota(jnp.int32, (height, both), 1)
        same = (row & (part - 1)) == (column & (part - 1))
        slot = along((1, both), 1, shift, values)
        return slot, jnp.logical_and((row >> shift) == slot, same).astype(jnp.float32)

    column_slot, taken = chosen_rows(tall, slots_to(1 - here, 0))
    _, summed = chosen_rows(tall, slots_to(1 - here, 1))
    outward = half(matrix_rows(both, (1 - here) * held), here)
    outward = jnp.where(column_slot < 0, outward, 0.0).astype(jnp.bfloat16)
    picks[...] = (taken + jnp.dot(
        summed.astype(jnp.bfloat16), outward, preferred_element_type=jnp.float32)).astype(jnp.bfloat16)
    pack(1)

    field_copy(0).wait()
    lower_block(0)
    for at in range(group + 2 * REACH + 1, 4 * group):
        lower_block(at)
    spread(2)
    near(2).start()
    field_copy(3).wait()
    lower(groups - 1)

    to_left = pltpu.make_async_remote_copy(
        src_ref=low.at[pl.ds(REACH, REACH)], dst_ref=low.at[pl.ds(REACH + count, REACH)],
        send_sem=halo_send.at[0], recv_sem=halo_recv.at[0],
        device_id={"mesh": slab - 1}, device_id_type=MESH)
    to_right = pltpu.make_async_remote_copy(
        src_ref=low.at[pl.ds(count, REACH)], dst_ref=low.at[pl.ds(0, REACH)],
        send_sem=halo_send.at[1], recv_sem=halo_recv.at[1],
        device_id={"mesh": slab + 1}, device_id_type=MESH)

    @pl.when(has_left)
    def _():
        to_left.start()

    @pl.when(has_right)
    def _():
        to_right.start()

    @pl.when(jnp.logical_not(has_left))
    def _():
        low[pl.ds(0, REACH)] = jnp.zeros((REACH, rows, size), jnp.bfloat16)

    @pl.when(jnp.logical_not(has_right))
    def _():
        low[pl.ds(REACH + count, REACH)] = jnp.zeros((REACH, rows, size), jnp.bfloat16)

    field_copy(1).wait()
    field_copy(2).wait()

    @pl.loop(2, groups)
    def _(t):
        g = turn(t)

        @pl.when(t + 2 <= groups - 2)
        def _():
            lower(t + 2)

        @pl.when(jnp.logical_and(t == groups - 2, has_right))
        def _():
            to_left.wait_recv()

        @pl.when(jnp.logical_and(t == groups - 1, has_left))
        def _():
            to_right.wait_recv()

        spread(g)
        near(g).start()
        pack(turn(t - 1))

    mine = matrix_rows(rows, me * (held // 2))
    _, arriving = chosen_rows(tall, slots_to(here, 0))
    inward = lax.dot_general(
        half(mine, 1 - here).astype(jnp.bfloat16), arriving.astype(jnp.bfloat16), (((1,), (1,)), ((), ())),
        preferred_element_type=jnp.float32)
    in_rows = slots_to(here, 1)
    my_slots = [jnp.where(core == 0, in_rows[i], in_rows[i + held // 2]) for i in range(held // 2)]
    row = lax.broadcasted_iota(jnp.int32, (rows, tall), 0)
    column = lax.broadcasted_iota(jnp.int32, (rows, tall), 1)
    own = jnp.logical_and(
        (column >> shift) == along((rows, 1), 0, shift, my_slots), (row & (part - 1)) == (column & (part - 1)))
    matrix[:, 0:both] = half(mine, here).astype(jnp.bfloat16)
    matrix[:, both:both + tall] = (inward + own.astype(jnp.float32)).astype(jnp.bfloat16)

    pack(turn(groups - 1))

    def forward(g):
        far(g).wait_recv()
        relay(g).start()

    later_copy.wait()
    right_copy.wait()
    ahead = groups // 2

    @pl.loop(0, groups)
    def _(t):
        @pl.when(lax.rem(t, 2) == 0)
        def _():
            forward(turn(t // 2))

        sums = stencil(t, later)
        for b in range(group):
            at = t * group + b
            cols = pl.ds(pl.multiple_of(at * size, size), size)
            rbuf[:, cols] = rbuf[:, cols] - sums[b * rows:(b + 1) * rows] * coef[0:1, cols]

    @pl.loop(0, groups)
    def _(t):
        @pl.when(jnp.logical_and(t + 1 >= ahead, t + 1 < groups))
        def _():
            forward(turn(t + 1))

        g = turn(t)
        relay(g).wait_recv()
        for b in range(group):
            at = g * group + b
            cols = pl.ds(pl.multiple_of(at * size, size), size)
            stacked = jnp.concatenate([gathered[:, at].reshape(both, size), arrived[at]], axis=0)
            mixed = jnp.dot(matrix[...], stacked, preferred_element_type=jnp.float32)
            left = rbuf[:, cols] - mixed
            rbuf[:, cols] = left
            fbuf[:, cols] = fbuf[:, cols] + scale[:, cols] * left

    def drain(source, sem, other):
        pltpu.make_async_remote_copy(
            src_ref=source, dst_ref=source, send_sem=sem, recv_sem=far_recv.at[0],
            device_id={"mode": other}, device_id_type=MESH).wait_send()

    drain(gathered.at[core], near_send, sibling)
    drain(outgoing, far_send, peer)
    drain(outgoing, forward_send, sibling)

    @pl.when(has_left)
    def _():
        to_left.wait_send()

    @pl.when(has_right)
    def _():
        to_right.wait_send()


def write_kernel(pieces, kept, found, updated, residual, sems):
    tall = kept.shape[0] // pieces
    for i in range(pieces):
        some = pl.ds(i * tall, tall)
        pltpu.make_async_copy(found.at[some], residual.at[some], sems.at[0]).start()
        pltpu.make_async_copy(kept.at[some], updated.at[some], sems.at[1]).start()
    pltpu.make_async_copy(found, residual, sems.at[0]).wait()
    pltpu.make_async_copy(kept, updated, sems.at[1]).wait()


def finish_kernel(pieces, field, found, precond, updated, residual, stage, sems):
    rows, width = field.shape
    span = width // pieces

    def columns(i):
        return pl.ds(pl.multiple_of(i * span, span), span)

    def found_copy(i):
        return pltpu.make_async_copy(found.at[:, columns(i)], residual.at[:, columns(i)], sems.at[0, i])

    def stage_copy(i):
        return pltpu.make_async_copy(stage.at[:, columns(i)], updated.at[:, columns(i)], sems.at[1, i])

    @pl.loop(0, pieces)
    def _(i):
        found_copy(i).start()
        cols = columns(i)
        stage[:, cols] = field[:, cols] + precond[:, cols] * found[:, cols]
        stage_copy(i).start()

    @pl.loop(0, pieces)
    def _(i):
        found_copy(i).wait()
        stage_copy(i).wait()


def shards(modes, slabs, field, right_side, coefficient, precond, blocks, couplings, chaos_values, chaos_index):
    rows, width = field.shape
    size = blocks.shape[-1]
    taps = blocks.shape[1]
    count = width // size
    group = 4
    groups = count // group
    others = max(modes // 2 - 1, 1)
    inside = pl.BlockSpec(memory_space=pltpu.VMEM)
    anywhere = pl.BlockSpec(memory_space=pl.ANY)
    spare = 67043328 - 2 * rows * width * 4 - 96 * 1024
    scalars = pl.BlockSpec(memory_space=pltpu.SMEM)
    dma = pltpu.SemaphoreType.DMA
    part = chaos_values.shape[1]
    both = 2 * rows
    entries = chaos_values.shape[0]
    common = [
        pltpu.VMEM((count + 2 * REACH, rows, size), jnp.bfloat16),
        pltpu.VMEM(blocks.shape, jnp.bfloat16),
        pltpu.VMEM(coefficient.shape, jnp.float32),
    ]
    waits = [dma((groups,)), dma((groups,)), dma((2,)), dma, dma((2,)), dma((2,))]
    arrays = [pltpu.VMEM((rows, width), jnp.float32)] * 2
    results = [jax.ShapeDtypeStruct((rows, width), jnp.float32)] * 2
    weights_row = precond[None, :]
    links = chaos_index.T
    values = chaos_values.transpose(1, 2, 0)

    def whole():
        kept, found = pl.pallas_call(
            functools.partial(kernel, modes, slabs, group),
            out_shape=arrays,
            in_specs=[anywhere, anywhere, anywhere, anywhere, scalars, inside, scalars],
            out_specs=[inside] * 2,
            scratch_shapes=common + [
                pltpu.VMEM((modes, count, rows, size), jnp.bfloat16),
                pltpu.VMEM((rows, modes * rows), jnp.bfloat16),
                pltpu.VMEM((max(entries, rows), modes * rows), jnp.float32),
            ] + waits + [dma((groups,)), dma((others, groups)), dma((others, groups)), dma((modes, groups))],
            compiler_params=pltpu.CompilerParams(
                collective_id=0, has_side_effects=True, vmem_limit_bytes=spare),
            name="gather_mix",
        )(field, right_side, coefficient, blocks, couplings.T, values, links)
        pieces = 16
        return tuple(pl.pallas_call(
            functools.partial(finish_kernel, pieces),
            out_shape=results,
            in_specs=[inside] * 3,
            out_specs=[anywhere] * 2,
            scratch_shapes=[pltpu.VMEM((rows, width), jnp.float32), dma((2, pieces))],
            compiler_params=pltpu.CompilerParams(vmem_limit_bytes=8 * 1024 * 1024),
            name="finish",
        )(kept, found, weights_row))

    held = both // part
    if modes != 4 or both % part or held != 8 or part & (part - 1) or groups % 4 or groups < 8:
        return whole()
    fewest = held // 2
    near_blocks = group + 2 * REACH

    prepared = pl.pallas_call(
        functools.partial(choose_kernel, group, fewest),
        out_shape=[
            jax.ShapeDtypeStruct((1, 1), jnp.int32),
            jax.ShapeDtypeStruct((1, 4 * held), jnp.int32),
            pltpu.VMEM(blocks.shape[1:], jnp.bfloat16),
            pltpu.VMEM((rows, near_blocks * size), jnp.float32),
            pltpu.VMEM(coefficient.shape, jnp.float32),
            pltpu.VMEM((1, width), jnp.float32),
            pltpu.VMEM((part * entries, 2 * both), jnp.bfloat16),
        ],
        in_specs=[anywhere] * 7,
        out_specs=[scalars, scalars] + [inside] * 5,
        scratch_shapes=[
            pltpu.VMEM(values.shape, jnp.bfloat16),
            pltpu.VMEM(links.shape, jnp.int32),
            pltpu.SMEM(links.shape, jnp.int32),
            dma((7,)),
        ],
        compiler_params=pltpu.CompilerParams(vmem_limit_bytes=67043328 - 4 * 1024 * 1024),
        name="choose",
    )(field, coefficient, weights_row, blocks, values, links, links)

    def reduced(packed, *operands):
        tall = packed * part
        kept, found = pl.pallas_call(
            functools.partial(packed_kernel, modes, slabs, group, entries, packed),
            out_shape=arrays,
            in_specs=[anywhere] * 5 + [inside] * 5,
            out_specs=[inside] * 2,
            scratch_shapes=[
                pltpu.VMEM((count + 2 * REACH, rows, size), jnp.bfloat16),
                pltpu.VMEM(blocks.shape[1:], jnp.bfloat16),
                pltpu.VMEM((2, count, rows, size), jnp.bfloat16),
                pltpu.VMEM((count // 2, tall, size), jnp.bfloat16),
                pltpu.VMEM((count, tall, size), jnp.bfloat16),
                pltpu.VMEM((tall, both), jnp.bfloat16),
                pltpu.VMEM((rows, both + tall), jnp.bfloat16),
                pltpu.SMEM((taps, count), jnp.int32),
                pltpu.SMEM((1, 4 * held), jnp.int32),
                dma((4,)), dma((4,)), dma((2,)), dma((2,)),
                dma, dma((groups,)), dma, dma((groups,)), dma, dma((groups,)),
            ],
            compiler_params=pltpu.CompilerParams(
                collective_id=packed, has_side_effects=True, vmem_limit_bytes=spare - 4 * 1024 * 1024),
            name="gather_mix",
        )(*operands)
        return tuple(pl.pallas_call(
            functools.partial(write_kernel, 8),
            out_shape=results,
            in_specs=[inside] * 2,
            out_specs=[anywhere] * 2,
            scratch_shapes=[dma((2,))],
            compiler_params=pltpu.CompilerParams(vmem_limit_bytes=8 * 1024 * 1024),
            name="write",
        )(kept, found))

    return lax.switch(
        prepared[0][0, 0],
        [functools.partial(reduced, packed) for packed in range(fewest, held + 1)],
        field, right_side, blocks, couplings.T, *prepared[1:])


def solution(mesh):
    placed = (
        P("mode", "mesh"),
        P("mode", "mesh"),
        P(None, "mesh"),
        P("mesh"),
        P(),
        P("mesh", None),
        P(),
        P(),
    )
    return jax.shard_map(
        functools.partial(shards, mesh.shape["mode"], mesh.shape["mesh"]),
        mesh=mesh,
        in_specs=placed,
        out_specs=(P("mode", "mesh"), P("mode", "mesh")),
        check_vma=False,
    )
```

```python
import functools

import jax
import jax.numpy as jnp
from jax import lax
from jax.experimental import pallas as pl
from jax.experimental.pallas import tpu as pltpu
from jax._src.lax.control_flow.conditionals import _switch_internal
from jax.sharding import PartitionSpec as P

MESH = pl.DeviceIdType.MESH
REACH = 3


def kernel(
    modes, slabs, group,
    field, right, coefficient, blocks, couplings, chaos_values, chaos_index,
    fbuf, rbuf,
    low, weights, coef, gathered, matrix, hits,
    field_sem, right_sem, weight_sem, coef_sem,
    halo_send, halo_recv, near_send, far_send, forward_send, recv,
):
    rows, width = field.shape
    size = blocks.shape[-1]
    count = width // size
    groups = count // group
    span = group * size
    taps = 2 * REACH + 1
    pairs = modes // 2
    me = lax.axis_index("mode")
    slab = lax.axis_index("mesh")
    sibling = me + 1 - 2 * lax.rem(me, 2)
    peers = [lax.rem(me + 2 * j, modes) for j in range(1, pairs)]
    has_left = slab > 0
    has_right = slab < slabs - 1

    def columns(g):
        return pl.ds(pl.multiple_of(g * span, span), span)

    def field_copy(g):
        return pltpu.make_async_copy(field.at[:, columns(g)], fbuf.at[:, columns(g)], field_sem.at[g])

    def right_copy(g):
        return pltpu.make_async_copy(right.at[:, columns(g)], rbuf.at[:, columns(g)], right_sem.at[g])

    def weight_copy(k):
        return pltpu.make_async_copy(blocks.at[k], weights.at[k], weight_sem.at[k])

    field_copy(0).start()
    field_copy(groups - 1).start()
    weight_copy(1).start()
    coef_copy = pltpu.make_async_copy(coefficient, coef, coef_sem)
    coef_copy.start()

    @pl.loop(1, groups - 1)
    def _(g):
        field_copy(g).start()

    weight_copy(0).start()

    @pl.loop(0, groups)
    def _(g):
        right_copy(g).start()

    barrier = pltpu.get_barrier_semaphore()
    for other in [sibling] + peers:
        pl.semaphore_signal(barrier, inc=1, device_id={"mode": other}, device_id_type=MESH)

    @pl.when(has_left)
    def _():
        pl.semaphore_signal(barrier, inc=1, device_id={"mesh": slab - 1}, device_id_type=MESH)

    @pl.when(has_right)
    def _():
        pl.semaphore_signal(barrier, inc=1, device_id={"mesh": slab + 1}, device_id_type=MESH)

    def lower(g):
        for b in range(group):
            at = g * group + b
            cols = pl.ds(pl.multiple_of(at * size, size), size)
            low[REACH + at] = fbuf[:, cols].astype(jnp.bfloat16)

    field_copy(0).wait()
    lower(0)
    field_copy(groups - 1).wait()
    lower(groups - 1)

    pl.semaphore_wait(barrier, pairs + jnp.minimum(slab, 1) + jnp.minimum(slabs - 1 - slab, 1))

    to_left = pltpu.make_async_remote_copy(
        src_ref=low.at[pl.ds(REACH, REACH)], dst_ref=low.at[pl.ds(REACH + count, REACH)],
        send_sem=halo_send.at[0], recv_sem=halo_recv.at[0],
        device_id={"mesh": slab - 1}, device_id_type=MESH)
    to_right = pltpu.make_async_remote_copy(
        src_ref=low.at[pl.ds(count, REACH)], dst_ref=low.at[pl.ds(0, REACH)],
        send_sem=halo_send.at[1], recv_sem=halo_recv.at[1],
        device_id={"mesh": slab + 1}, device_id_type=MESH)

    @pl.when(has_left)
    def _():
        to_left.start()

    @pl.when(has_right)
    def _():
        to_right.start()

    @pl.when(jnp.logical_not(has_left))
    def _():
        low[pl.ds(0, REACH)] = jnp.zeros((REACH, rows, size), jnp.bfloat16)

    @pl.when(jnp.logical_not(has_right))
    def _():
        low[pl.ds(REACH + count, REACH)] = jnp.zeros((REACH, rows, size), jnp.bfloat16)

    field_copy(1).wait()
    lower(1)
    weight_copy(1).wait()
    coef_copy.wait()

    def stencil(g, k):
        tall = []
        for b in range(group):
            at = g * group + b
            wide = []
            for c in range(taps):
                keep = jnp.full((rows, size), couplings[c, at].astype(jnp.float32)).astype(jnp.bfloat16)
                wide.append(low[at + c] * keep)
            tall.append(jnp.concatenate(wide, axis=1))
        stacked = jnp.concatenate(tall, axis=0)
        return jnp.dot(stacked, weights[k].reshape(taps * size, size), preferred_element_type=jnp.float32)

    def piece(slot, g):
        return gathered.at[slot, pl.ds(g * group, group)]

    def send(slot, g, target, sem):
        return pltpu.make_async_remote_copy(
            src_ref=piece(slot, g), dst_ref=piece(slot, g), send_sem=sem, recv_sem=recv.at[slot, g],
            device_id={"mode": target}, device_id_type=MESH)

    def turn(t):
        return lax.rem(t + 1, groups)

    @pl.loop(0, groups)
    def _(t):
        g = turn(t)

        @pl.when(t + 2 <= groups - 2)
        def _():
            field_copy(t + 2).wait()
            lower(t + 2)

        @pl.when(jnp.logical_and(t == groups - 2, has_right))
        def _():
            to_left.wait_recv()

        @pl.when(jnp.logical_and(t == groups - 1, has_left))
        def _():
            to_right.wait_recv()

        sums = stencil(g, 1)
        for b in range(group):
            at = g * group + b
            cols = pl.ds(pl.multiple_of(at * size, size), size)
            scaled = sums[b * rows:(b + 1) * rows] * coef[1:2, cols]
            gathered[me, at] = scaled.astype(jnp.bfloat16)
        for j, peer in enumerate(peers):
            send(me, g, peer, far_send.at[j, g]).start()
        send(me, g, sibling, near_send.at[g]).start()

    part, _, links = chaos_values.shape
    total_rows = modes * rows
    per_row = links * part // total_rows
    column_of = lax.broadcasted_iota(jnp.int32, (1, total_rows), 1) // part
    for n in range(links):
        hits[n:n + 1, :] = (column_of == chaos_index[1, n]).astype(jnp.float32)
    lane_of = lax.broadcasted_iota(jnp.int32, (part, total_rows), 1)
    step_of = lax.broadcasted_iota(jnp.int32, (part, total_rows), 0)
    repeat = (lax.rem(lane_of, part) == step_of).astype(jnp.float32).astype(jnp.bfloat16)
    row_of = lax.broadcasted_iota(jnp.int32, (rows, links), 0)
    owner_of = lax.broadcasted_iota(jnp.int32, (rows, links), 1) // per_row
    owned = owner_of == row_of // part + me * (rows // part)
    built = jnp.zeros((rows, total_rows), jnp.float32)
    for i in range(part):
        spread_out = lax.dot_general(
            chaos_values[i], repeat, (((0,), (0,)), ((), ())), preferred_element_type=jnp.float32)
        placed = (spread_out * hits[0:links, :]).astype(jnp.bfloat16)
        mine = jnp.logical_and(owned, lax.rem(row_of, part) == i).astype(jnp.float32).astype(jnp.bfloat16)
        built = built + jnp.dot(mine, placed, preferred_element_type=jnp.float32)
    matrix[...] = built.astype(jnp.bfloat16)

    weight_copy(0).wait()

    @pl.loop(0, groups)
    def _(t):
        g = turn(t)
        right_copy(g).wait()
        sums = stencil(g, 0)
        for b in range(group):
            at = g * group + b
            cols = pl.ds(pl.multiple_of(at * size, size), size)
            rbuf[:, cols] = rbuf[:, cols] - sums[b * rows:(b + 1) * rows] * coef[0:1, cols]

    def mix(g):
        send(sibling, g, sibling, near_send.at[g]).wait_recv()
        for j, peer in enumerate(peers):
            other = peer + 1 - 2 * lax.rem(peer, 2)
            send(other, g, sibling, forward_send.at[j, g]).wait_recv()
        for b in range(group):
            at = g * group + b
            cols = pl.ds(pl.multiple_of(at * size, size), size)
            mixed = jnp.dot(
                matrix[...], gathered[:, at].reshape(modes * rows, size), preferred_element_type=jnp.float32)
            rbuf[:, cols] = rbuf[:, cols] - mixed

    def forward(g):
        for j, peer in enumerate(peers):
            send(peer, g, peer, far_send.at[j, g]).wait_recv()
            send(peer, g, sibling, forward_send.at[j, g]).start()

    forward(turn(0))

    @pl.loop(1, groups)
    def _(t):
        forward(turn(t))
        mix(turn(t - 1))

    mix(turn(groups - 1))

    @pl.loop(0, groups)
    def _(g):
        send(me, g, sibling, near_send.at[g]).wait_send()
        for j, peer in enumerate(peers):
            send(me, g, peer, far_send.at[j, g]).wait_send()
            send(peer, g, sibling, forward_send.at[j, g]).wait_send()

    @pl.when(has_left)
    def _():
        to_left.wait_send()

    @pl.when(has_right)
    def _():
        to_right.wait_send()


def masked_stencil(low, base, couplings, at, group, weights, taps, size):
    rows = low.shape[1]
    tall = []
    for b in range(group):
        wide = []
        for c in range(taps):
            keep = jnp.full((rows, size), couplings[c, at + b].astype(jnp.float32)).astype(jnp.bfloat16)
            wide.append(low[base + b + c] * keep)
        tall.append(jnp.concatenate(wide, axis=1))
    stacked = jnp.concatenate(tall, axis=0)
    return jnp.dot(stacked, weights.reshape(taps * size, size), preferred_element_type=jnp.float32)


def cheapest_cover(held, adjacent):
    chosen = lax.broadcasted_iota(jnp.int32, (8, 128), 0) * 128 + lax.broadcasted_iota(jnp.int32, (8, 128), 1)
    rest = chosen ^ (2 ** held - 1)
    columns = sum((chosen >> i) & 1 for i in range(held))
    uncovered = sum(jnp.where((rest & links) != 0, 1, 0) for links in adjacent)
    key = ((columns + uncovered) << (held + 4)) + (uncovered << held) + chosen
    key = jnp.where(chosen < 2 ** held, key.astype(jnp.float32), float(2 ** 23))
    return jnp.min(key).astype(jnp.int32)


def slots_of(held, chosen, adjacent):
    used = jnp.int32(0)
    columns = []
    for c in range(held):
        taken = (chosen >> c) & 1
        columns.append(jnp.where(taken == 1, used, -1))
        used = used + taken
    rows = []
    for links in adjacent:
        taken = jnp.where((links & ~chosen) != 0, 1, 0)
        rows.append(jnp.where(taken == 1, used, -1))
        used = used + taken
    return columns, rows


def along(shape, axis, shift, values):
    block = lax.broadcasted_iota(jnp.int32, shape, axis) >> shift
    found = jnp.full(shape, -1, jnp.int32)
    for i, value in enumerate(values):
        found = jnp.where(block == i, value, found)
    return found


def choose_kernel(
    group, fewest,
    field, coefficient, precond, blocks, couplings, chaos_values, chaos_index, index_row,
    choice, slots, kept_links, weights, first, coef, scale, placed,
    values, wide_index, links_smem, sems,
):
    size = blocks.shape[-1]
    part, _, entries = chaos_values.shape
    total = placed.shape[1]
    held = total // part // 2
    shift = held.bit_length() - 1
    per_row = entries // (2 * held)
    near_span = pl.ds((group - REACH) * size, (group + 2 * REACH) * size)
    index_copy = pltpu.make_async_copy(chaos_index, links_smem, sems.at[0])
    row_copy = pltpu.make_async_copy(index_row, wide_index, sems.at[1])
    values_copy = pltpu.make_async_copy(chaos_values, values, sems.at[2])
    coef_copy = pltpu.make_async_copy(coefficient, coef, sems.at[3])
    scale_copy = pltpu.make_async_copy(precond, scale, sems.at[4])
    kept_copy = pltpu.make_async_copy(couplings, kept_links, sems.at[7])
    index_copy.start()
    row_copy.start()
    values_copy.start()
    kept_copy.start()
    tiles = first.shape[0] // 8
    for i in range(tiles):
        pltpu.make_async_copy(
            field.at[pl.ds(i * 8, 8), near_span], first.at[pl.ds(i * 8, 8)], sems.at[5]).start()
    for i in range(weights.shape[0]):
        pltpu.make_async_copy(blocks.at[1, i], weights.at[i], sems.at[6]).start()
    coef_copy.start()
    scale_copy.start()

    index_copy.wait()
    adjacent = [[], []]
    for row in range(2 * held):
        side = row // held
        links = jnp.int32(0)
        for n in range(row * per_row, row * per_row + per_row):
            column = links_smem[1, n]
            links = links | (((column >> shift) ^ side) << (column & (held - 1)))
        adjacent[side].append(links)
    best = [cheapest_cover(held, links) for links in adjacent]
    inward = best[0] >> (held + 4)
    needed = jnp.maximum(jnp.maximum(inward, best[1] >> (held + 4)), fewest)
    choice[0, 0] = 2 * (needed - fewest) + jnp.where(inward < needed, 1, 0)
    for side in range(2):
        columns, rows = slots_of(held, best[side] & (2 ** held - 1), adjacent[side])
        for i, value in enumerate(columns + rows):
            slots[0, side * 2 * held + i] = value

    row_copy.wait()
    values_copy.wait()
    square = (entries, entries)
    wide_row = jnp.broadcast_to(wide_index[1:2, :], square).astype(jnp.float32)
    eye = lax.broadcasted_iota(jnp.int32, square, 0) == lax.broadcasted_iota(jnp.int32, square, 1)
    column_of = jnp.sum(jnp.where(eye, wide_row, 0.0), axis=1, keepdims=True)
    step = part.bit_length() - 1
    lane_block = (lax.broadcasted_iota(jnp.int32, (entries, total), 1) >> step).astype(jnp.float32)
    hits = (lane_block == column_of).astype(jnp.float32)
    lane_of = lax.broadcasted_iota(jnp.int32, (part, total), 1)
    step_of = lax.broadcasted_iota(jnp.int32, (part, total), 0)
    repeat = ((lane_of & (part - 1)) == step_of).astype(jnp.float32).astype(jnp.bfloat16)
    for i in range(part):
        spread_out = lax.dot_general(
            values[i], repeat, (((0,), (0,)), ((), ())), preferred_element_type=jnp.float32)
        placed[i * entries:(i + 1) * entries] = (spread_out * hits).astype(jnp.bfloat16)

    pltpu.make_async_copy(field.at[:, near_span], first, sems.at[5]).wait()
    pltpu.make_async_copy(blocks.at[1], weights, sems.at[6]).wait()
    coef_copy.wait()
    scale_copy.wait()
    kept_copy.wait()


def packed_kernel(
    modes, slabs, group, entries, packed, lean,
    field, right, blocks, slot_of, links, early, first, coef, scale, placed,
    fbuf, rbuf,
    low, later, gathered, outgoing, arrived, picks, matrix,
    load_sem, field_sem, halo_send, halo_recv,
    near_send, near_recv, far_send, far_recv, forward_send, forward_recv,
):
    rows, width = field.shape
    size = blocks.shape[-1]
    count = width // size
    groups = count // group
    span = group * size
    taps = 2 * REACH + 1
    pairs = modes // 2
    both = 2 * rows
    total = 2 * both
    part = picks.shape[0] // packed
    held = both // part
    shift = part.bit_length() - 1
    per_row = entries // (2 * held)
    tall = packed * part
    small = tall - part if lean else tall
    me = lax.axis_index("mode")
    slab = lax.axis_index("mesh")
    sibling = me + 1 - 2 * lax.rem(me, 2)
    peer = lax.rem(me + 2, modes)
    core = lax.rem(me, 2)
    here = me // 2
    share = group // 2
    batch = groups // 4
    has_left = slab > 0
    has_right = slab < slabs - 1

    barrier = pltpu.get_barrier_semaphore()
    for other in [sibling, peer]:
        pl.semaphore_signal(barrier, inc=1, device_id={"mode": other}, device_id_type=MESH)

    @pl.when(has_left)
    def _():
        pl.semaphore_signal(barrier, inc=1, device_id={"mesh": slab - 1}, device_id_type=MESH)

    @pl.when(has_right)
    def _():
        pl.semaphore_signal(barrier, inc=1, device_id={"mesh": slab + 1}, device_id_type=MESH)

    def field_copy(q):
        cols = pl.ds(pl.multiple_of(q * batch * span, span), batch * span)
        return pltpu.make_async_copy(field.at[:, cols], fbuf.at[:, cols], field_sem.at[q])

    later_copy = pltpu.make_async_copy(blocks.at[0], later, load_sem.at[0])
    right_copy = pltpu.make_async_copy(right, rbuf, load_sem.at[1])
    for q in (0, 3, 1, 2):
        field_copy(q).start()
    later_copy.start()
    right_copy.start()

    def lower_block(at):
        cols = pl.ds(pl.multiple_of(at * size, size), size)
        low[REACH + at] = fbuf[:, cols].astype(jnp.bfloat16)

    def lower(g):
        for b in range(group):
            lower_block(g * group + b)

    def near(g):
        ours = gathered.at[core, pl.ds(g * group, group)]
        return pltpu.make_async_remote_copy(
            src_ref=ours, dst_ref=ours, send_sem=near_send, recv_sem=near_recv.at[g],
            device_id={"mode": sibling}, device_id_type=MESH)

    def far(g, height):
        return pltpu.make_async_remote_copy(
            src_ref=outgoing.at[pl.ds(g * share, share), pl.ds(0, height)],
            dst_ref=arrived.at[pl.ds(g * group + core * share, share), pl.ds(0, height)],
            send_sem=far_send, recv_sem=far_recv.at[g],
            device_id={"mode": peer}, device_id_type=MESH)

    def relay(g, height):
        ours = arrived.at[pl.ds(g * group + core * share, share), pl.ds(0, height)]
        return pltpu.make_async_remote_copy(
            src_ref=ours, dst_ref=ours, send_sem=forward_send, recv_sem=forward_recv.at[g],
            device_id={"mode": sibling}, device_id_type=MESH)

    def sized(lean_side, act):
        if not lean:
            act(tall)
            return

        @pl.when(here == lean_side)
        def _():
            act(small)

        @pl.when(here != lean_side)
        def _():
            act(tall)

    def pack(g):
        near(g).wait_recv()
        for b in range(share):
            at = g * group + core * share + b
            outgoing[g * share + b] = jnp.dot(
                picks[...], gathered[:, at].reshape(both, size),
                preferred_element_type=jnp.float32).astype(jnp.bfloat16)
        sized(1, lambda height: far(g, height).start())

    def turn(t):
        return lax.rem(t + 1, groups)

    def stencil(g, weights):
        return masked_stencil(low, g * group, links, g * group, group, weights[...], taps, size)

    def spread(g):
        sums = stencil(g, early)
        for b in range(group):
            at = g * group + b
            cols = pl.ds(pl.multiple_of(at * size, size), size)
            scaled = sums[b * rows:(b + 1) * rows] * coef[1:2, cols]
            gathered[core, at] = scaled.astype(jnp.bfloat16)

    for b in range(group + 2 * REACH):
        low[group + b] = first[:, b * size:(b + 1) * size].astype(jnp.bfloat16)

    to_left = pltpu.make_async_remote_copy(
        src_ref=low.at[pl.ds(REACH, REACH)], dst_ref=low.at[pl.ds(REACH + count, REACH)],
        send_sem=halo_send.at[0], recv_sem=halo_recv.at[0],
        device_id={"mesh": slab - 1}, device_id_type=MESH)
    to_right = pltpu.make_async_remote_copy(
        src_ref=low.at[pl.ds(count, REACH)], dst_ref=low.at[pl.ds(0, REACH)],
        send_sem=halo_send.at[1], recv_sem=halo_recv.at[1],
        device_id={"mesh": slab + 1}, device_id_type=MESH)

    lane = lax.broadcasted_iota(jnp.int32, (1, part * entries), 1)
    lane_step = lax.div(lane, entries)
    lane_key = lane_step * 2 * held + lax.div(lane - lane_step * entries, per_row)

    def matrix_rows(height, start):
        row = lax.broadcasted_iota(jnp.int32, (height, 1), 0)
        row_key = (row & (part - 1)) * 2 * held + (row >> shift) + start
        wanted = (row_key == lane_key).astype(jnp.float32).astype(jnp.bfloat16)
        return jnp.dot(wanted, placed[...], preferred_element_type=jnp.float32)

    def half(values, side):
        return jnp.where(side == 0, values[:, 0:both], values[:, both:total])

    def slots_to(side, kind):
        first_slot = [slot_of[0, kind * held + i] for i in range(held)]
        other_slot = [slot_of[0, (2 + kind) * held + i] for i in range(held)]
        return [jnp.where(side == 0, a, b) for a, b in zip(first_slot, other_slot)]

    def chosen_rows(height, values):
        row = lax.broadcasted_iota(jnp.int32, (height, both), 0)
        column = lax.broadcasted_iota(jnp.int32, (height, both), 1)
        same = (row & (part - 1)) == (column & (part - 1))
        slot = along((1, both), 1, shift, values)
        return slot, jnp.logical_and((row >> shift) == slot, same).astype(jnp.float32)

    @pl.loop(0, groups + 1)
    def _(t):
        g = turn(t)

        @pl.when(t == 1)
        def _():
            field_copy(0).wait()

            @pl.loop(0, 4 * group)
            def _(at):
                lower_block(at)

        @pl.when(jnp.logical_and(t >= 2, t + 2 <= groups - 2))
        def _():
            lower(t + 2)

        @pl.when(jnp.logical_and(t == groups - 2, has_right))
        def _():
            to_left.wait_recv()

        @pl.when(jnp.logical_and(t == groups - 1, has_left))
        def _():
            to_right.wait_recv()

        @pl.when(t < groups)
        def _():
            spread(g)

            @pl.when(t == 0)
            def _():
                pl.semaphore_wait(barrier, pairs + jnp.minimum(slab, 1) + jnp.minimum(slabs - 1 - slab, 1))

            near(g).start()

        @pl.when(t == 0)
        def _():
            column_slot, taken = chosen_rows(tall, slots_to(1 - here, 0))
            _, summed = chosen_rows(tall, slots_to(1 - here, 1))
            outward = half(matrix_rows(both, (1 - here) * held), here)
            outward = jnp.where(column_slot < 0, outward, 0.0).astype(jnp.bfloat16)
            picks[...] = (taken + jnp.dot(
                summed.astype(jnp.bfloat16), outward, preferred_element_type=jnp.float32)).astype(jnp.bfloat16)

        @pl.when(t > 0)
        def _():
            pack(turn(t - 1))

        @pl.when(t == 1)
        def _():
            field_copy(3).wait()
            lower(groups - 1)

            @pl.when(has_left)
            def _():
                to_left.start()

            @pl.when(has_right)
            def _():
                to_right.start()

            @pl.when(jnp.logical_not(has_left))
            def _():
                low[pl.ds(0, REACH)] = jnp.zeros((REACH, rows, size), jnp.bfloat16)

            @pl.when(jnp.logical_not(has_right))
            def _():
                low[pl.ds(REACH + count, REACH)] = jnp.zeros((REACH, rows, size), jnp.bfloat16)

            field_copy(1).wait()
            field_copy(2).wait()


    later_copy.wait()
    mine = matrix_rows(rows, me * (held // 2))
    _, arriving = chosen_rows(tall, slots_to(here, 0))
    inward = lax.dot_general(
        half(mine, 1 - here).astype(jnp.bfloat16), arriving.astype(jnp.bfloat16), (((1,), (1,)), ((), ())),
        preferred_element_type=jnp.float32)
    in_rows = slots_to(here, 1)
    my_slots = [jnp.where(core == 0, in_rows[i], in_rows[i + held // 2]) for i in range(held // 2)]
    row = lax.broadcasted_iota(jnp.int32, (rows, tall), 0)
    column = lax.broadcasted_iota(jnp.int32, (rows, tall), 1)
    own = jnp.logical_and(
        (column >> shift) == along((rows, 1), 0, shift, my_slots), (row & (part - 1)) == (column & (part - 1)))
    matrix[:, 0:both] = half(mine, here).astype(jnp.bfloat16)
    matrix[:, both:both + tall] = (inward + own.astype(jnp.float32)).astype(jnp.bfloat16)

    if lean:
        @pl.when(here == 0)
        def _():
            @pl.loop(0, count)
            def _(at):
                arrived[at, small:tall] = jnp.zeros((part, size), jnp.bfloat16)

    def forward(g):
        def act(height):
            far(g, height).wait_recv()
            relay(g, height).start()

        sized(0, act)

    right_copy.wait()
    ahead = groups // 2

    @pl.loop(0, groups)
    def _(t):
        @pl.when(lax.rem(t, 2) == 0)
        def _():
            forward(turn(t // 2))

        sums = stencil(t, later)
        for b in range(group):
            at = t * group + b
            cols = pl.ds(pl.multiple_of(at * size, size), size)
            rbuf[:, cols] = rbuf[:, cols] - sums[b * rows:(b + 1) * rows] * coef[0:1, cols]

    @pl.loop(0, groups)
    def _(t):
        @pl.when(jnp.logical_and(t + 1 >= ahead, t + 1 < groups))
        def _():
            forward(turn(t + 1))

        g = turn(t)
        sized(0, lambda height: relay(g, height).wait_recv())
        for b in range(group):
            at = g * group + b
            cols = pl.ds(pl.multiple_of(at * size, size), size)
            stacked = jnp.concatenate([gathered[:, at].reshape(both, size), arrived[at]], axis=0)
            mixed = jnp.dot(matrix[...], stacked, preferred_element_type=jnp.float32)
            left = rbuf[:, cols] - mixed
            rbuf[:, cols] = left
            fbuf[:, cols] = fbuf[:, cols] + scale[:, cols] * left

    def drain(source, sem, other):
        pltpu.make_async_remote_copy(
            src_ref=source, dst_ref=source, send_sem=sem, recv_sem=far_recv.at[0],
            device_id={"mode": other}, device_id_type=MESH).wait_send()

    drain(gathered.at[core], near_send, sibling)
    sized(1, lambda height: drain(outgoing.at[:, pl.ds(0, height)], far_send, peer))
    sized(0, lambda height: drain(outgoing.at[:, pl.ds(0, height)], forward_send, sibling))

    @pl.when(has_left)
    def _():
        to_left.wait_send()

    @pl.when(has_right)
    def _():
        to_right.wait_send()


def write_kernel(pieces, kept, found, updated, residual, sems):
    tall = kept.shape[0] // pieces
    for i in range(pieces):
        some = pl.ds(i * tall, tall)
        pltpu.make_async_copy(found.at[some], residual.at[some], sems.at[0]).start()
        pltpu.make_async_copy(kept.at[some], updated.at[some], sems.at[1]).start()
    pltpu.make_async_copy(found, residual, sems.at[0]).wait()
    pltpu.make_async_copy(kept, updated, sems.at[1]).wait()


def finish_kernel(pieces, field, found, precond, updated, residual, stage, sems):
    rows, width = field.shape
    span = width // pieces

    def columns(i):
        return pl.ds(pl.multiple_of(i * span, span), span)

    def found_copy(i):
        return pltpu.make_async_copy(found.at[:, columns(i)], residual.at[:, columns(i)], sems.at[0, i])

    def stage_copy(i):
        return pltpu.make_async_copy(stage.at[:, columns(i)], updated.at[:, columns(i)], sems.at[1, i])

    @pl.loop(0, pieces)
    def _(i):
        found_copy(i).start()
        cols = columns(i)
        stage[:, cols] = field[:, cols] + precond[:, cols] * found[:, cols]
        stage_copy(i).start()

    @pl.loop(0, pieces)
    def _(i):
        found_copy(i).wait()
        stage_copy(i).wait()


def shards(modes, slabs, field, right_side, coefficient, precond, blocks, couplings, chaos_values, chaos_index):
    rows, width = field.shape
    size = blocks.shape[-1]
    taps = blocks.shape[1]
    count = width // size
    group = 4
    groups = count // group
    others = max(modes // 2 - 1, 1)
    inside = pl.BlockSpec(memory_space=pltpu.VMEM)
    anywhere = pl.BlockSpec(memory_space=pl.ANY)
    spare = 67043328 - 2 * rows * width * 4 - 96 * 1024
    scalars = pl.BlockSpec(memory_space=pltpu.SMEM)
    dma = pltpu.SemaphoreType.DMA
    part = chaos_values.shape[1]
    both = 2 * rows
    entries = chaos_values.shape[0]
    common = [
        pltpu.VMEM((count + 2 * REACH, rows, size), jnp.bfloat16),
        pltpu.VMEM(blocks.shape, jnp.bfloat16),
        pltpu.VMEM(coefficient.shape, jnp.float32),
    ]
    waits = [dma((groups,)), dma((groups,)), dma((2,)), dma, dma((2,)), dma((2,))]
    arrays = [pltpu.VMEM((rows, width), jnp.float32)] * 2
    results = [jax.ShapeDtypeStruct((rows, width), jnp.float32)] * 2
    weights_row = precond[None, :]
    links = chaos_index.T
    values = chaos_values.transpose(1, 2, 0)

    def whole():
        kept, found = pl.pallas_call(
            functools.partial(kernel, modes, slabs, group),
            out_shape=arrays,
            in_specs=[anywhere, anywhere, anywhere, anywhere, scalars, inside, scalars],
            out_specs=[inside] * 2,
            scratch_shapes=common + [
                pltpu.VMEM((modes, count, rows, size), jnp.bfloat16),
                pltpu.VMEM((rows, modes * rows), jnp.bfloat16),
                pltpu.VMEM((max(entries, rows), modes * rows), jnp.float32),
            ] + waits + [dma((groups,)), dma((others, groups)), dma((others, groups)), dma((modes, groups))],
            compiler_params=pltpu.CompilerParams(
                collective_id=0, has_side_effects=True, vmem_limit_bytes=spare),
            name="gather_mix",
        )(field, right_side, coefficient, blocks, couplings.T, values, links)
        pieces = 16
        return tuple(pl.pallas_call(
            functools.partial(finish_kernel, pieces),
            out_shape=results,
            in_specs=[inside] * 3,
            out_specs=[anywhere] * 2,
            scratch_shapes=[pltpu.VMEM((rows, width), jnp.float32), dma((2, pieces))],
            compiler_params=pltpu.CompilerParams(vmem_limit_bytes=8 * 1024 * 1024),
            name="finish",
        )(kept, found, weights_row))

    held = both // part
    if modes != 4 or both % part or held != 8 or part & (part - 1) or groups % 4 or groups < 8:
        return whole()
    fewest = held // 2
    near_blocks = group + 2 * REACH

    prepared = pl.pallas_call(
        functools.partial(choose_kernel, group, fewest),
        out_shape=[
            pltpu.SMEM((1, 1), jnp.int32),
            pltpu.SMEM((1, 4 * held), jnp.int32),
            pltpu.SMEM((taps, count), jnp.int32),
            pltpu.VMEM(blocks.shape[1:], jnp.bfloat16),
            pltpu.VMEM((rows, near_blocks * size), jnp.float32),
            pltpu.VMEM(coefficient.shape, jnp.float32),
            pltpu.VMEM((1, width), jnp.float32),
            pltpu.VMEM((part * entries, 2 * both), jnp.bfloat16),
        ],
        in_specs=[anywhere] * 8,
        out_specs=[scalars] * 3 + [inside] * 5,
        scratch_shapes=[
            pltpu.VMEM(values.shape, jnp.bfloat16),
            pltpu.VMEM(links.shape, jnp.int32),
            pltpu.SMEM(links.shape, jnp.int32),
            dma((8,)),
        ],
        compiler_params=pltpu.CompilerParams(vmem_limit_bytes=67043328 - 5 * 512 * 1024),
        name="choose",
    )(field, coefficient, weights_row, blocks, couplings.T, values, links, links)

    def reduced(packed, lean, *operands):
        tall = packed * part
        kept, found = pl.pallas_call(
            functools.partial(packed_kernel, modes, slabs, group, entries, packed, lean),
            out_shape=arrays,
            in_specs=[anywhere] * 3 + [scalars] * 2 + [inside] * 5,
            out_specs=[inside] * 2,
            scratch_shapes=[
                pltpu.VMEM((count + 2 * REACH, rows, size), jnp.bfloat16),
                pltpu.VMEM(blocks.shape[1:], jnp.bfloat16),
                pltpu.VMEM((2, count, rows, size), jnp.bfloat16),
                pltpu.VMEM((count // 2, tall, size), jnp.bfloat16),
                pltpu.VMEM((count, tall, size), jnp.bfloat16),
                pltpu.VMEM((tall, both), jnp.bfloat16),
                pltpu.VMEM((rows, both + tall), jnp.bfloat16),
                dma((2,)), dma((4,)), dma((2,)), dma((2,)),
                dma, dma((groups,)), dma, dma((groups,)), dma, dma((groups,)),
            ],
            compiler_params=pltpu.CompilerParams(
                collective_id=2 * packed + lean, has_side_effects=True, vmem_limit_bytes=spare - 4 * 1024 * 1024),
            name="gather_mix",
        )(*operands)
        return tuple(pl.pallas_call(
            functools.partial(write_kernel, 8),
            out_shape=results,
            in_specs=[inside] * 2,
            out_specs=[anywhere] * 2,
            scratch_shapes=[dma((2,))],
            compiler_params=pltpu.CompilerParams(vmem_limit_bytes=8 * 1024 * 1024),
            name="write",
        )(kept, found))

    return _switch_internal(
        prepared[0][0, 0],
        [functools.partial(reduced, packed, lean) for packed in range(fewest, held + 1) for lean in (False, True)],
        (field, right_side, blocks, *prepared[1:]), branches_platforms=None)


def solution(mesh):
    placed = (
        P("mode", "mesh"),
        P("mode", "mesh"),
        P(None, "mesh"),
        P("mesh"),
        P(),
        P("mesh", None),
        P(),
        P(),
    )
    return jax.shard_map(
        functools.partial(shards, mesh.shape["mode"], mesh.shape["mesh"]),
        mesh=mesh,
        in_specs=placed,
        out_specs=(P("mode", "mesh"), P("mode", "mesh")),
        check_vma=False,
    )
```

```python
import functools

import jax
import jax.numpy as jnp
from jax import lax
from jax.experimental import pallas as pl
from jax.experimental.pallas import tpu as pltpu
from jax._src.lax.control_flow.conditionals import _switch_internal
from jax.sharding import PartitionSpec as P

MESH = pl.DeviceIdType.MESH
REACH = 3


def kernel(
    modes, slabs, group,
    field, right, coefficient, blocks, couplings, chaos_values, chaos_index,
    fbuf, rbuf,
    low, weights, coef, gathered, matrix, hits,
    field_sem, right_sem, weight_sem, coef_sem,
    halo_send, halo_recv, near_send, far_send, forward_send, recv,
):
    rows, width = field.shape
    size = blocks.shape[-1]
    count = width // size
    groups = count // group
    span = group * size
    taps = 2 * REACH + 1
    pairs = modes // 2
    me = lax.axis_index("mode")
    slab = lax.axis_index("mesh")
    sibling = me + 1 - 2 * lax.rem(me, 2)
    peers = [lax.rem(me + 2 * j, modes) for j in range(1, pairs)]
    has_left = slab > 0
    has_right = slab < slabs - 1

    def columns(g):
        return pl.ds(pl.multiple_of(g * span, span), span)

    def field_copy(g):
        return pltpu.make_async_copy(field.at[:, columns(g)], fbuf.at[:, columns(g)], field_sem.at[g])

    def right_copy(g):
        return pltpu.make_async_copy(right.at[:, columns(g)], rbuf.at[:, columns(g)], right_sem.at[g])

    def weight_copy(k):
        return pltpu.make_async_copy(blocks.at[k], weights.at[k], weight_sem.at[k])

    field_copy(0).start()
    field_copy(groups - 1).start()
    weight_copy(1).start()
    coef_copy = pltpu.make_async_copy(coefficient, coef, coef_sem)
    coef_copy.start()

    @pl.loop(1, groups - 1)
    def _(g):
        field_copy(g).start()

    weight_copy(0).start()

    @pl.loop(0, groups)
    def _(g):
        right_copy(g).start()

    barrier = pltpu.get_barrier_semaphore()
    for other in [sibling] + peers:
        pl.semaphore_signal(barrier, inc=1, device_id={"mode": other}, device_id_type=MESH)

    @pl.when(has_left)
    def _():
        pl.semaphore_signal(barrier, inc=1, device_id={"mesh": slab - 1}, device_id_type=MESH)

    @pl.when(has_right)
    def _():
        pl.semaphore_signal(barrier, inc=1, device_id={"mesh": slab + 1}, device_id_type=MESH)

    def lower(g):
        for b in range(group):
            at = g * group + b
            cols = pl.ds(pl.multiple_of(at * size, size), size)
            low[REACH + at] = fbuf[:, cols].astype(jnp.bfloat16)

    field_copy(0).wait()
    lower(0)
    field_copy(groups - 1).wait()
    lower(groups - 1)

    pl.semaphore_wait(barrier, pairs + jnp.minimum(slab, 1) + jnp.minimum(slabs - 1 - slab, 1))

    to_left = pltpu.make_async_remote_copy(
        src_ref=low.at[pl.ds(REACH, REACH)], dst_ref=low.at[pl.ds(REACH + count, REACH)],
        send_sem=halo_send.at[0], recv_sem=halo_recv.at[0],
        device_id={"mesh": slab - 1}, device_id_type=MESH)
    to_right = pltpu.make_async_remote_copy(
        src_ref=low.at[pl.ds(count, REACH)], dst_ref=low.at[pl.ds(0, REACH)],
        send_sem=halo_send.at[1], recv_sem=halo_recv.at[1],
        device_id={"mesh": slab + 1}, device_id_type=MESH)

    @pl.when(has_left)
    def _():
        to_left.start()

    @pl.when(has_right)
    def _():
        to_right.start()

    @pl.when(jnp.logical_not(has_left))
    def _():
        low[pl.ds(0, REACH)] = jnp.zeros((REACH, rows, size), jnp.bfloat16)

    @pl.when(jnp.logical_not(has_right))
    def _():
        low[pl.ds(REACH + count, REACH)] = jnp.zeros((REACH, rows, size), jnp.bfloat16)

    field_copy(1).wait()
    lower(1)
    weight_copy(1).wait()
    coef_copy.wait()

    def stencil(g, k):
        tall = []
        for b in range(group):
            at = g * group + b
            wide = []
            for c in range(taps):
                keep = jnp.full((rows, size), couplings[c, at].astype(jnp.float32)).astype(jnp.bfloat16)
                wide.append(low[at + c] * keep)
            tall.append(jnp.concatenate(wide, axis=1))
        stacked = jnp.concatenate(tall, axis=0)
        return jnp.dot(stacked, weights[k].reshape(taps * size, size), preferred_element_type=jnp.float32)

    def piece(slot, g):
        return gathered.at[slot, pl.ds(g * group, group)]

    def send(slot, g, target, sem):
        return pltpu.make_async_remote_copy(
            src_ref=piece(slot, g), dst_ref=piece(slot, g), send_sem=sem, recv_sem=recv.at[slot, g],
            device_id={"mode": target}, device_id_type=MESH)

    def turn(t):
        return lax.rem(t + 1, groups)

    @pl.loop(0, groups)
    def _(t):
        g = turn(t)

        @pl.when(t + 2 <= groups - 2)
        def _():
            field_copy(t + 2).wait()
            lower(t + 2)

        @pl.when(jnp.logical_and(t == groups - 2, has_right))
        def _():
            to_left.wait_recv()

        @pl.when(jnp.logical_and(t == groups - 1, has_left))
        def _():
            to_right.wait_recv()

        sums = stencil(g, 1)
        for b in range(group):
            at = g * group + b
            cols = pl.ds(pl.multiple_of(at * size, size), size)
            scaled = sums[b * rows:(b + 1) * rows] * coef[1:2, cols]
            gathered[me, at] = scaled.astype(jnp.bfloat16)
        for j, peer in enumerate(peers):
            send(me, g, peer, far_send.at[j, g]).start()
        send(me, g, sibling, near_send.at[g]).start()

    part, _, links = chaos_values.shape
    total_rows = modes * rows
    per_row = links * part // total_rows
    column_of = lax.broadcasted_iota(jnp.int32, (1, total_rows), 1) // part
    for n in range(links):
        hits[n:n + 1, :] = (column_of == chaos_index[1, n]).astype(jnp.float32)
    lane_of = lax.broadcasted_iota(jnp.int32, (part, total_rows), 1)
    step_of = lax.broadcasted_iota(jnp.int32, (part, total_rows), 0)
    repeat = (lax.rem(lane_of, part) == step_of).astype(jnp.float32).astype(jnp.bfloat16)
    row_of = lax.broadcasted_iota(jnp.int32, (rows, links), 0)
    owner_of = lax.broadcasted_iota(jnp.int32, (rows, links), 1) // per_row
    owned = owner_of == row_of // part + me * (rows // part)
    built = jnp.zeros((rows, total_rows), jnp.float32)
    for i in range(part):
        spread_out = lax.dot_general(
            chaos_values[i], repeat, (((0,), (0,)), ((), ())), preferred_element_type=jnp.float32)
        placed = (spread_out * hits[0:links, :]).astype(jnp.bfloat16)
        mine = jnp.logical_and(owned, lax.rem(row_of, part) == i).astype(jnp.float32).astype(jnp.bfloat16)
        built = built + jnp.dot(mine, placed, preferred_element_type=jnp.float32)
    matrix[...] = built.astype(jnp.bfloat16)

    weight_copy(0).wait()

    @pl.loop(0, groups)
    def _(t):
        g = turn(t)
        right_copy(g).wait()
        sums = stencil(g, 0)
        for b in range(group):
            at = g * group + b
            cols = pl.ds(pl.multiple_of(at * size, size), size)
            rbuf[:, cols] = rbuf[:, cols] - sums[b * rows:(b + 1) * rows] * coef[0:1, cols]

    def mix(g):
        send(sibling, g, sibling, near_send.at[g]).wait_recv()
        for j, peer in enumerate(peers):
            other = peer + 1 - 2 * lax.rem(peer, 2)
            send(other, g, sibling, forward_send.at[j, g]).wait_recv()
        for b in range(group):
            at = g * group + b
            cols = pl.ds(pl.multiple_of(at * size, size), size)
            mixed = jnp.dot(
                matrix[...], gathered[:, at].reshape(modes * rows, size), preferred_element_type=jnp.float32)
            rbuf[:, cols] = rbuf[:, cols] - mixed

    def forward(g):
        for j, peer in enumerate(peers):
            send(peer, g, peer, far_send.at[j, g]).wait_recv()
            send(peer, g, sibling, forward_send.at[j, g]).start()

    forward(turn(0))

    @pl.loop(1, groups)
    def _(t):
        forward(turn(t))
        mix(turn(t - 1))

    mix(turn(groups - 1))

    @pl.loop(0, groups)
    def _(g):
        send(me, g, sibling, near_send.at[g]).wait_send()
        for j, peer in enumerate(peers):
            send(me, g, peer, far_send.at[j, g]).wait_send()
            send(peer, g, sibling, forward_send.at[j, g]).wait_send()

    @pl.when(has_left)
    def _():
        to_left.wait_send()

    @pl.when(has_right)
    def _():
        to_right.wait_send()


def masked_stencil(low, base, couplings, at, group, weights, taps, size):
    rows = low.shape[1]
    tall = []
    for b in range(group):
        wide = []
        for c in range(taps):
            keep = jnp.full((rows, size), couplings[c, at + b].astype(jnp.float32)).astype(jnp.bfloat16)
            wide.append(low[base + b + c] * keep)
        tall.append(jnp.concatenate(wide, axis=1))
    stacked = jnp.concatenate(tall, axis=0)
    return jnp.dot(stacked, weights.reshape(taps * size, size), preferred_element_type=jnp.float32)


def cheapest_cover(held, adjacent):
    chosen = lax.broadcasted_iota(jnp.int32, (8, 128), 0) * 128 + lax.broadcasted_iota(jnp.int32, (8, 128), 1)
    rest = chosen ^ (2 ** held - 1)
    columns = sum((chosen >> i) & 1 for i in range(held))
    uncovered = sum(jnp.where((rest & links) != 0, 1, 0) for links in adjacent)
    key = ((columns + uncovered) << (held + 4)) + (uncovered << held) + chosen
    key = jnp.where(chosen < 2 ** held, key.astype(jnp.float32), float(2 ** 23))
    return jnp.min(key).astype(jnp.int32)


def slots_of(held, chosen, adjacent):
    used = jnp.int32(0)
    columns = []
    for c in range(held):
        taken = (chosen >> c) & 1
        columns.append(jnp.where(taken == 1, used, -1))
        used = used + taken
    rows = []
    for links in adjacent:
        taken = jnp.where((links & ~chosen) != 0, 1, 0)
        rows.append(jnp.where(taken == 1, used, -1))
        used = used + taken
    return columns, rows


def along(shape, axis, shift, values):
    block = lax.broadcasted_iota(jnp.int32, shape, axis) >> shift
    found = jnp.full(shape, -1, jnp.int32)
    for i, value in enumerate(values):
        found = jnp.where(block == i, value, found)
    return found


def choose_kernel(
    group, fewest,
    field, coefficient, precond, blocks, couplings, chaos_values, chaos_index, index_row,
    choice, slots, kept_links, weights, first, coef, scale, placed,
    values, wide_index, links_smem, sems,
):
    size = blocks.shape[-1]
    part, _, entries = chaos_values.shape
    total = placed.shape[1]
    held = total // part // 2
    shift = held.bit_length() - 1
    per_row = entries // (2 * held)
    near_span = pl.ds((group - REACH) * size, (group + 2 * REACH) * size)
    index_copy = pltpu.make_async_copy(chaos_index, links_smem, sems.at[0])
    row_copy = pltpu.make_async_copy(index_row, wide_index, sems.at[1])
    values_copy = pltpu.make_async_copy(chaos_values, values, sems.at[2])
    coef_copy = pltpu.make_async_copy(coefficient, coef, sems.at[3])
    scale_copy = pltpu.make_async_copy(precond, scale, sems.at[4])
    kept_copy = pltpu.make_async_copy(couplings, kept_links, sems.at[7])
    index_copy.start()
    row_copy.start()
    values_copy.start()
    kept_copy.start()
    tiles = first.shape[0] // 8
    for i in range(tiles):
        pltpu.make_async_copy(
            field.at[pl.ds(i * 8, 8), near_span], first.at[pl.ds(i * 8, 8)], sems.at[5]).start()
    for i in range(weights.shape[0]):
        pltpu.make_async_copy(blocks.at[1, i], weights.at[i], sems.at[6]).start()
    coef_copy.start()
    scale_copy.start()

    index_copy.wait()
    adjacent = [[], []]
    for row in range(2 * held):
        side = row // held
        links = jnp.int32(0)
        for n in range(row * per_row, row * per_row + per_row):
            column = links_smem[1, n]
            links = links | (((column >> shift) ^ side) << (column & (held - 1)))
        adjacent[side].append(links)
    best = [cheapest_cover(held, links) for links in adjacent]
    inward = best[0] >> (held + 4)
    needed = jnp.maximum(jnp.maximum(inward, best[1] >> (held + 4)), fewest)
    choice[0, 0] = 2 * (needed - fewest) + jnp.where(inward < needed, 1, 0)
    for side in range(2):
        columns, rows = slots_of(held, best[side] & (2 ** held - 1), adjacent[side])
        for i, value in enumerate(columns + rows):
            slots[0, side * 2 * held + i] = value

    row_copy.wait()
    values_copy.wait()
    square = (entries, entries)
    wide_row = jnp.broadcast_to(wide_index[1:2, :], square).astype(jnp.float32)
    eye = lax.broadcasted_iota(jnp.int32, square, 0) == lax.broadcasted_iota(jnp.int32, square, 1)
    column_of = jnp.sum(jnp.where(eye, wide_row, 0.0), axis=1, keepdims=True)
    step = part.bit_length() - 1
    lane_block = (lax.broadcasted_iota(jnp.int32, (entries, total), 1) >> step).astype(jnp.float32)
    hits = (lane_block == column_of).astype(jnp.float32)
    lane_of = lax.broadcasted_iota(jnp.int32, (part, total), 1)
    step_of = lax.broadcasted_iota(jnp.int32, (part, total), 0)
    repeat = ((lane_of & (part - 1)) == step_of).astype(jnp.float32).astype(jnp.bfloat16)
    for i in range(part):
        spread_out = lax.dot_general(
            values[i], repeat, (((0,), (0,)), ((), ())), preferred_element_type=jnp.float32)
        placed[i * entries:(i + 1) * entries] = (spread_out * hits).astype(jnp.bfloat16)

    pltpu.make_async_copy(field.at[:, near_span], first, sems.at[5]).wait()
    pltpu.make_async_copy(blocks.at[1], weights, sems.at[6]).wait()
    coef_copy.wait()
    scale_copy.wait()
    kept_copy.wait()


def packed_kernel(
    modes, slabs, group, entries, packed, lean,
    field, right, blocks, slot_of, links, early, first, coef, scale, placed,
    fbuf, rbuf,
    low, later, gathered, outgoing, arrived, picks, matrix,
    load_sem, field_sem, halo_send, halo_recv,
    near_send, near_recv, far_send, far_recv, forward_send, forward_recv,
):
    rows, width = field.shape
    size = blocks.shape[-1]
    count = width // size
    groups = count // group
    span = group * size
    taps = 2 * REACH + 1
    pairs = modes // 2
    both = 2 * rows
    total = 2 * both
    part = picks.shape[0] // packed
    held = both // part
    shift = part.bit_length() - 1
    per_row = entries // (2 * held)
    tall = packed * part
    small = tall - part if lean else tall
    me = lax.axis_index("mode")
    slab = lax.axis_index("mesh")
    sibling = me + 1 - 2 * lax.rem(me, 2)
    peer = lax.rem(me + 2, modes)
    core = lax.rem(me, 2)
    here = me // 2
    share = group // 2
    batch = groups // 4
    has_left = slab > 0
    has_right = slab < slabs - 1

    barrier = pltpu.get_barrier_semaphore()
    for other in [sibling, peer]:
        pl.semaphore_signal(barrier, inc=1, device_id={"mode": other}, device_id_type=MESH)

    @pl.when(has_left)
    def _():
        pl.semaphore_signal(barrier, inc=1, device_id={"mesh": slab - 1}, device_id_type=MESH)

    @pl.when(has_right)
    def _():
        pl.semaphore_signal(barrier, inc=1, device_id={"mesh": slab + 1}, device_id_type=MESH)

    def field_copy(q):
        cols = pl.ds(pl.multiple_of(q * batch * span, span), batch * span)
        return pltpu.make_async_copy(field.at[:, cols], fbuf.at[:, cols], field_sem.at[q])

    later_copy = pltpu.make_async_copy(blocks.at[0], later, load_sem.at[0])
    right_copy = pltpu.make_async_copy(right, rbuf, load_sem.at[1])
    for q in (0, 3, 1, 2):
        field_copy(q).start()
    later_copy.start()
    right_copy.start()

    def lower_block(at):
        cols = pl.ds(pl.multiple_of(at * size, size), size)
        low[REACH + at] = fbuf[:, cols].astype(jnp.bfloat16)

    def lower(g):
        for b in range(group):
            lower_block(g * group + b)

    def near(g):
        ours = gathered.at[core, pl.ds(g * group, group)]
        return pltpu.make_async_remote_copy(
            src_ref=ours, dst_ref=ours, send_sem=near_send, recv_sem=near_recv.at[g],
            device_id={"mode": sibling}, device_id_type=MESH)

    def far(g, height):
        return pltpu.make_async_remote_copy(
            src_ref=outgoing.at[pl.ds(g * share, share), pl.ds(0, height)],
            dst_ref=arrived.at[pl.ds(g * group + core * share, share), pl.ds(0, height)],
            send_sem=far_send, recv_sem=far_recv.at[g],
            device_id={"mode": peer}, device_id_type=MESH)

    def relay(g, height):
        ours = arrived.at[pl.ds(g * group + core * share, share), pl.ds(0, height)]
        return pltpu.make_async_remote_copy(
            src_ref=ours, dst_ref=ours, send_sem=forward_send, recv_sem=forward_recv.at[g],
            device_id={"mode": sibling}, device_id_type=MESH)

    def sized(lean_side, act):
        if not lean:
            act(tall)
            return

        @pl.when(here == lean_side)
        def _():
            act(small)

        @pl.when(here != lean_side)
        def _():
            act(tall)

    def pack(g):
        near(g).wait_recv()
        for b in range(share):
            at = g * group + core * share + b
            outgoing[g * share + b] = jnp.dot(
                picks[...], gathered[:, at].reshape(both, size),
                preferred_element_type=jnp.float32).astype(jnp.bfloat16)
        sized(1, lambda height: far(g, height).start())

    def turn(t):
        return lax.rem(t + 1, groups)

    def stencil(g, weights):
        return masked_stencil(low, g * group, links, g * group, group, weights[...], taps, size)

    def spread(g):
        sums = stencil(g, early)
        for b in range(group):
            at = g * group + b
            cols = pl.ds(pl.multiple_of(at * size, size), size)
            scaled = sums[b * rows:(b + 1) * rows] * coef[1:2, cols]
            gathered[core, at] = scaled.astype(jnp.bfloat16)

    for b in range(group + 2 * REACH):
        low[group + b] = first[:, b * size:(b + 1) * size].astype(jnp.bfloat16)

    to_left = pltpu.make_async_remote_copy(
        src_ref=low.at[pl.ds(REACH, REACH)], dst_ref=low.at[pl.ds(REACH + count, REACH)],
        send_sem=halo_send.at[0], recv_sem=halo_recv.at[0],
        device_id={"mesh": slab - 1}, device_id_type=MESH)
    to_right = pltpu.make_async_remote_copy(
        src_ref=low.at[pl.ds(count, REACH)], dst_ref=low.at[pl.ds(0, REACH)],
        send_sem=halo_send.at[1], recv_sem=halo_recv.at[1],
        device_id={"mesh": slab + 1}, device_id_type=MESH)

    lane = lax.broadcasted_iota(jnp.int32, (1, part * entries), 1)
    lane_step = lax.div(lane, entries)
    lane_key = lane_step * 2 * held + lax.div(lane - lane_step * entries, per_row)

    def matrix_rows(height, start):
        row = lax.broadcasted_iota(jnp.int32, (height, 1), 0)
        row_key = (row & (part - 1)) * 2 * held + (row >> shift) + start
        wanted = (row_key == lane_key).astype(jnp.float32).astype(jnp.bfloat16)
        return jnp.dot(wanted, placed[...], preferred_element_type=jnp.float32)

    def half(values, side):
        return jnp.where(side == 0, values[:, 0:both], values[:, both:total])

    def slots_to(side, kind):
        first_slot = [slot_of[0, kind * held + i] for i in range(held)]
        other_slot = [slot_of[0, (2 + kind) * held + i] for i in range(held)]
        return [jnp.where(side == 0, a, b) for a, b in zip(first_slot, other_slot)]

    def chosen_rows(height, values):
        row = lax.broadcasted_iota(jnp.int32, (height, both), 0)
        column = lax.broadcasted_iota(jnp.int32, (height, both), 1)
        same = (row & (part - 1)) == (column & (part - 1))
        slot = along((1, both), 1, shift, values)
        return slot, jnp.logical_and((row >> shift) == slot, same).astype(jnp.float32)

    @pl.loop(0, groups + 1)
    def _(t):
        g = turn(t)

        @pl.when(t == 1)
        def _():
            field_copy(0).wait()
            for at in range(group + group + REACH, 4 * group):
                lower_block(at)

        @pl.when(jnp.logical_and(t >= 2, t + 2 <= groups - 2))
        def _():
            lower(t + 2)

        @pl.when(jnp.logical_and(t == groups - 2, has_right))
        def _():
            to_left.wait_recv()

        @pl.when(jnp.logical_and(t == groups - 1, has_left))
        def _():
            to_right.wait_recv()

        @pl.when(t < groups)
        def _():
            spread(g)

            @pl.when(t == 0)
            def _():
                pl.semaphore_wait(barrier, pairs + jnp.minimum(slab, 1) + jnp.minimum(slabs - 1 - slab, 1))

            near(g).start()

        @pl.when(t == 0)
        def _():
            column_slot, taken = chosen_rows(tall, slots_to(1 - here, 0))
            _, summed = chosen_rows(tall, slots_to(1 - here, 1))
            outward = half(matrix_rows(both, (1 - here) * held), here)
            outward = jnp.where(column_slot < 0, outward, 0.0).astype(jnp.bfloat16)
            picks[...] = (taken + jnp.dot(
                summed.astype(jnp.bfloat16), outward, preferred_element_type=jnp.float32)).astype(jnp.bfloat16)

        @pl.when(t != 1)
        def _():
            pack(turn(jnp.maximum(t - 1, 0)))

        @pl.when(t == 1)
        def _():
            lower_block(0)
            field_copy(3).wait()
            lower(groups - 1)

            @pl.when(has_left)
            def _():
                to_left.start()

            @pl.when(has_right)
            def _():
                to_right.start()

            @pl.when(jnp.logical_not(has_left))
            def _():
                low[pl.ds(0, REACH)] = jnp.zeros((REACH, rows, size), jnp.bfloat16)

            @pl.when(jnp.logical_not(has_right))
            def _():
                low[pl.ds(REACH + count, REACH)] = jnp.zeros((REACH, rows, size), jnp.bfloat16)

            field_copy(1).wait()
            field_copy(2).wait()


    later_copy.wait()
    mine = matrix_rows(rows, me * (held // 2))
    _, arriving = chosen_rows(tall, slots_to(here, 0))
    inward = lax.dot_general(
        half(mine, 1 - here).astype(jnp.bfloat16), arriving.astype(jnp.bfloat16), (((1,), (1,)), ((), ())),
        preferred_element_type=jnp.float32)
    in_rows = slots_to(here, 1)
    my_slots = [jnp.where(core == 0, in_rows[i], in_rows[i + held // 2]) for i in range(held // 2)]
    row = lax.broadcasted_iota(jnp.int32, (rows, tall), 0)
    column = lax.broadcasted_iota(jnp.int32, (rows, tall), 1)
    own = jnp.logical_and(
        (column >> shift) == along((rows, 1), 0, shift, my_slots), (row & (part - 1)) == (column & (part - 1)))
    matrix[:, 0:both] = half(mine, here).astype(jnp.bfloat16)
    matrix[:, both:both + tall] = (inward + own.astype(jnp.float32)).astype(jnp.bfloat16)

    if lean:
        @pl.when(here == 0)
        def _():
            @pl.loop(0, count)
            def _(at):
                arrived[at, small:tall] = jnp.zeros((part, size), jnp.bfloat16)

    def forward(g):
        def act(height):
            far(g, height).wait_recv()
            relay(g, height).start()

        sized(0, act)

    right_copy.wait()
    ahead = groups // 2

    wide = 2 * group

    @pl.loop(0, groups // 2)
    def _(t):
        forward(turn(t))
        base = t * wide
        sums = masked_stencil(low, base, links, base, wide, later[...], taps, size)
        for b in range(wide):
            cols = pl.ds(pl.multiple_of((base + b) * size, size), size)
            rbuf[:, cols] = rbuf[:, cols] - sums[b * rows:(b + 1) * rows] * coef[0:1, cols]

    @pl.loop(0, groups)
    def _(t):
        @pl.when(jnp.logical_and(t + 1 >= ahead, t + 1 < groups))
        def _():
            forward(turn(t + 1))

        g = turn(t)
        sized(0, lambda height: relay(g, height).wait_recv())
        for b in range(group):
            at = g * group + b
            cols = pl.ds(pl.multiple_of(at * size, size), size)
            stacked = jnp.concatenate([gathered[:, at].reshape(both, size), arrived[at]], axis=0)
            mixed = jnp.dot(matrix[...], stacked, preferred_element_type=jnp.float32)
            left = rbuf[:, cols] - mixed
            rbuf[:, cols] = left
            fbuf[:, cols] = fbuf[:, cols] + scale[:, cols] * left

    def drain(source, sem, other):
        pltpu.make_async_remote_copy(
            src_ref=source, dst_ref=source, send_sem=sem, recv_sem=far_recv.at[0],
            device_id={"mode": other}, device_id_type=MESH).wait_send()

    drain(gathered.at[core], near_send, sibling)
    sized(1, lambda height: drain(outgoing.at[:, pl.ds(0, height)], far_send, peer))
    sized(0, lambda height: drain(outgoing.at[:, pl.ds(0, height)], forward_send, sibling))

    @pl.when(has_left)
    def _():
        to_left.wait_send()

    @pl.when(has_right)
    def _():
        to_right.wait_send()


def write_kernel(pieces, kept, found, updated, residual, sems):
    span = kept.shape[1] // pieces

    @pl.loop(0, pieces)
    def _(i):
        some = pl.ds(pl.multiple_of(i * span, span), span)
        pltpu.make_async_copy(found.at[:, some], residual.at[:, some], sems.at[0]).start()
        pltpu.make_async_copy(kept.at[:, some], updated.at[:, some], sems.at[1]).start()

    pltpu.make_async_copy(found, residual, sems.at[0]).wait()
    pltpu.make_async_copy(kept, updated, sems.at[1]).wait()


def finish_kernel(pieces, field, found, precond, updated, residual, stage, sems):
    rows, width = field.shape
    span = width // pieces

    def columns(i):
        return pl.ds(pl.multiple_of(i * span, span), span)

    def found_copy(i):
        return pltpu.make_async_copy(found.at[:, columns(i)], residual.at[:, columns(i)], sems.at[0, i])

    def stage_copy(i):
        return pltpu.make_async_copy(stage.at[:, columns(i)], updated.at[:, columns(i)], sems.at[1, i])

    @pl.loop(0, pieces)
    def _(i):
        found_copy(i).start()
        cols = columns(i)
        stage[:, cols] = field[:, cols] + precond[:, cols] * found[:, cols]
        stage_copy(i).start()

    @pl.loop(0, pieces)
    def _(i):
        found_copy(i).wait()
        stage_copy(i).wait()


def shards(modes, slabs, field, right_side, coefficient, precond, blocks, couplings, chaos_values, chaos_index):
    rows, width = field.shape
    size = blocks.shape[-1]
    taps = blocks.shape[1]
    count = width // size
    group = 4
    groups = count // group
    others = max(modes // 2 - 1, 1)
    inside = pl.BlockSpec(memory_space=pltpu.VMEM)
    anywhere = pl.BlockSpec(memory_space=pl.ANY)
    spare = 67043328 - 2 * rows * width * 4 - 96 * 1024
    scalars = pl.BlockSpec(memory_space=pltpu.SMEM)
    dma = pltpu.SemaphoreType.DMA
    part = chaos_values.shape[1]
    both = 2 * rows
    entries = chaos_values.shape[0]
    common = [
        pltpu.VMEM((count + 2 * REACH, rows, size), jnp.bfloat16),
        pltpu.VMEM(blocks.shape, jnp.bfloat16),
        pltpu.VMEM(coefficient.shape, jnp.float32),
    ]
    waits = [dma((groups,)), dma((groups,)), dma((2,)), dma, dma((2,)), dma((2,))]
    arrays = [pltpu.VMEM((rows, width), jnp.float32)] * 2
    results = [jax.ShapeDtypeStruct((rows, width), jnp.float32)] * 2
    weights_row = precond[None, :]
    links = chaos_index.T
    values = chaos_values.transpose(1, 2, 0)

    def whole():
        kept, found = pl.pallas_call(
            functools.partial(kernel, modes, slabs, group),
            out_shape=arrays,
            in_specs=[anywhere, anywhere, anywhere, anywhere, scalars, inside, scalars],
            out_specs=[inside] * 2,
            scratch_shapes=common + [
                pltpu.VMEM((modes, count, rows, size), jnp.bfloat16),
                pltpu.VMEM((rows, modes * rows), jnp.bfloat16),
                pltpu.VMEM((max(entries, rows), modes * rows), jnp.float32),
            ] + waits + [dma((groups,)), dma((others, groups)), dma((others, groups)), dma((modes, groups))],
            compiler_params=pltpu.CompilerParams(
                collective_id=0, has_side_effects=True, vmem_limit_bytes=spare),
            name="gather_mix",
        )(field, right_side, coefficient, blocks, couplings.T, values, links)
        pieces = 16
        return tuple(pl.pallas_call(
            functools.partial(finish_kernel, pieces),
            out_shape=results,
            in_specs=[inside] * 3,
            out_specs=[anywhere] * 2,
            scratch_shapes=[pltpu.VMEM((rows, width), jnp.float32), dma((2, pieces))],
            compiler_params=pltpu.CompilerParams(vmem_limit_bytes=8 * 1024 * 1024),
            name="finish",
        )(kept, found, weights_row))

    held = both // part
    if modes != 4 or both % part or held != 8 or part & (part - 1) or groups % 4 or groups < 8:
        return whole()
    fewest = held // 2
    near_blocks = group + 2 * REACH

    prepared = pl.pallas_call(
        functools.partial(choose_kernel, group, fewest),
        out_shape=[
            pltpu.SMEM((1, 1), jnp.int32),
            pltpu.SMEM((1, 4 * held), jnp.int32),
            pltpu.SMEM((taps, count), jnp.int32),
            pltpu.VMEM(blocks.shape[1:], jnp.bfloat16),
            pltpu.VMEM((rows, near_blocks * size), jnp.float32),
            pltpu.VMEM(coefficient.shape, jnp.float32),
            pltpu.VMEM((1, width), jnp.float32),
            pltpu.VMEM((part * entries, 2 * both), jnp.bfloat16),
        ],
        in_specs=[anywhere] * 8,
        out_specs=[scalars] * 3 + [inside] * 5,
        scratch_shapes=[
            pltpu.VMEM(values.shape, jnp.bfloat16),
            pltpu.VMEM(links.shape, jnp.int32),
            pltpu.SMEM(links.shape, jnp.int32),
            dma((8,)),
        ],
        compiler_params=pltpu.CompilerParams(vmem_limit_bytes=67043328 - 5 * 512 * 1024),
        name="choose",
    )(field, coefficient, weights_row, blocks, couplings.T, values, links, links)

    def reduced(packed, lean, *operands):
        tall = packed * part
        kept, found = pl.pallas_call(
            functools.partial(packed_kernel, modes, slabs, group, entries, packed, lean),
            out_shape=arrays,
            in_specs=[anywhere] * 3 + [scalars] * 2 + [inside] * 5,
            out_specs=[inside] * 2,
            scratch_shapes=[
                pltpu.VMEM((count + 2 * REACH, rows, size), jnp.bfloat16),
                pltpu.VMEM(blocks.shape[1:], jnp.bfloat16),
                pltpu.VMEM((2, count, rows, size), jnp.bfloat16),
                pltpu.VMEM((count // 2, tall, size), jnp.bfloat16),
                pltpu.VMEM((count, tall, size), jnp.bfloat16),
                pltpu.VMEM((tall, both), jnp.bfloat16),
                pltpu.VMEM((rows, both + tall), jnp.bfloat16),
                dma((2,)), dma((4,)), dma((2,)), dma((2,)),
                dma, dma((groups,)), dma, dma((groups,)), dma, dma((groups,)),
            ],
            compiler_params=pltpu.CompilerParams(
                collective_id=2 * packed + lean, has_side_effects=True, vmem_limit_bytes=spare - 4 * 1024 * 1024),
            name="gather_mix",
        )(*operands)
        return tuple(pl.pallas_call(
            functools.partial(write_kernel, count),
            out_shape=results,
            in_specs=[inside] * 2,
            out_specs=[anywhere] * 2,
            scratch_shapes=[dma((2,))],
            compiler_params=pltpu.CompilerParams(vmem_limit_bytes=8 * 1024 * 1024),
            name="write",
        )(kept, found))

    return _switch_internal(
        prepared[0][0, 0],
        [functools.partial(reduced, packed, lean) for packed in range(fewest, held + 1) for lean in (False, True)],
        (field, right_side, blocks, *prepared[1:]), branches_platforms=None)


def solution(mesh):
    placed = (
        P("mode", "mesh"),
        P("mode", "mesh"),
        P(None, "mesh"),
        P("mesh"),
        P(),
        P("mesh", None),
        P(),
        P(),
    )
    return jax.shard_map(
        functools.partial(shards, mesh.shape["mode"], mesh.shape["mesh"]),
        mesh=mesh,
        in_specs=placed,
        out_specs=(P("mode", "mesh"), P("mode", "mesh")),
        check_vma=False,
    )
```

```python
import functools

import jax
import jax.numpy as jnp
from jax import lax
from jax.experimental import pallas as pl
from jax.experimental.pallas import tpu as pltpu
from jax._src.lax.control_flow.conditionals import _switch_internal
from jax.sharding import PartitionSpec as P

MESH = pl.DeviceIdType.MESH
REACH = 3


def kernel(
    modes, slabs, group,
    field, right, coefficient, blocks, couplings, chaos_values, chaos_index,
    fbuf, rbuf,
    low, weights, coef, gathered, matrix, hits,
    field_sem, right_sem, weight_sem, coef_sem,
    halo_send, halo_recv, near_send, far_send, forward_send, recv,
):
    rows, width = field.shape
    size = blocks.shape[-1]
    count = width // size
    groups = count // group
    span = group * size
    taps = 2 * REACH + 1
    pairs = modes // 2
    me = lax.axis_index("mode")
    slab = lax.axis_index("mesh")
    sibling = me + 1 - 2 * lax.rem(me, 2)
    peers = [lax.rem(me + 2 * j, modes) for j in range(1, pairs)]
    has_left = slab > 0
    has_right = slab < slabs - 1

    def columns(g):
        return pl.ds(pl.multiple_of(g * span, span), span)

    def field_copy(g):
        return pltpu.make_async_copy(field.at[:, columns(g)], fbuf.at[:, columns(g)], field_sem.at[g])

    def right_copy(g):
        return pltpu.make_async_copy(right.at[:, columns(g)], rbuf.at[:, columns(g)], right_sem.at[g])

    def weight_copy(k):
        return pltpu.make_async_copy(blocks.at[k], weights.at[k], weight_sem.at[k])

    field_copy(0).start()
    field_copy(groups - 1).start()
    weight_copy(1).start()
    coef_copy = pltpu.make_async_copy(coefficient, coef, coef_sem)
    coef_copy.start()

    @pl.loop(1, groups - 1)
    def _(g):
        field_copy(g).start()

    weight_copy(0).start()

    @pl.loop(0, groups)
    def _(g):
        right_copy(g).start()

    barrier = pltpu.get_barrier_semaphore()
    for other in [sibling] + peers:
        pl.semaphore_signal(barrier, inc=1, device_id={"mode": other}, device_id_type=MESH)

    @pl.when(has_left)
    def _():
        pl.semaphore_signal(barrier, inc=1, device_id={"mesh": slab - 1}, device_id_type=MESH)

    @pl.when(has_right)
    def _():
        pl.semaphore_signal(barrier, inc=1, device_id={"mesh": slab + 1}, device_id_type=MESH)

    def lower(g):
        for b in range(group):
            at = g * group + b
            cols = pl.ds(pl.multiple_of(at * size, size), size)
            low[REACH + at] = fbuf[:, cols].astype(jnp.bfloat16)

    field_copy(0).wait()
    lower(0)
    field_copy(groups - 1).wait()
    lower(groups - 1)

    pl.semaphore_wait(barrier, pairs + jnp.minimum(slab, 1) + jnp.minimum(slabs - 1 - slab, 1))

    to_left = pltpu.make_async_remote_copy(
        src_ref=low.at[pl.ds(REACH, REACH)], dst_ref=low.at[pl.ds(REACH + count, REACH)],
        send_sem=halo_send.at[0], recv_sem=halo_recv.at[0],
        device_id={"mesh": slab - 1}, device_id_type=MESH)
    to_right = pltpu.make_async_remote_copy(
        src_ref=low.at[pl.ds(count, REACH)], dst_ref=low.at[pl.ds(0, REACH)],
        send_sem=halo_send.at[1], recv_sem=halo_recv.at[1],
        device_id={"mesh": slab + 1}, device_id_type=MESH)

    @pl.when(has_left)
    def _():
        to_left.start()

    @pl.when(has_right)
    def _():
        to_right.start()

    @pl.when(jnp.logical_not(has_left))
    def _():
        low[pl.ds(0, REACH)] = jnp.zeros((REACH, rows, size), jnp.bfloat16)

    @pl.when(jnp.logical_not(has_right))
    def _():
        low[pl.ds(REACH + count, REACH)] = jnp.zeros((REACH, rows, size), jnp.bfloat16)

    field_copy(1).wait()
    lower(1)
    weight_copy(1).wait()
    coef_copy.wait()

    def stencil(g, k):
        tall = []
        for b in range(group):
            at = g * group + b
            wide = []
            for c in range(taps):
                keep = jnp.full((rows, size), couplings[c, at].astype(jnp.float32)).astype(jnp.bfloat16)
                wide.append(low[at + c] * keep)
            tall.append(jnp.concatenate(wide, axis=1))
        stacked = jnp.concatenate(tall, axis=0)
        return jnp.dot(stacked, weights[k].reshape(taps * size, size), preferred_element_type=jnp.float32)

    def piece(slot, g):
        return gathered.at[slot, pl.ds(g * group, group)]

    def send(slot, g, target, sem):
        return pltpu.make_async_remote_copy(
            src_ref=piece(slot, g), dst_ref=piece(slot, g), send_sem=sem, recv_sem=recv.at[slot, g],
            device_id={"mode": target}, device_id_type=MESH)

    def turn(t):
        return lax.rem(t + 1, groups)

    @pl.loop(0, groups)
    def _(t):
        g = turn(t)

        @pl.when(t + 2 <= groups - 2)
        def _():
            field_copy(t + 2).wait()
            lower(t + 2)

        @pl.when(jnp.logical_and(t == groups - 2, has_right))
        def _():
            to_left.wait_recv()

        @pl.when(jnp.logical_and(t == groups - 1, has_left))
        def _():
            to_right.wait_recv()

        sums = stencil(g, 1)
        for b in range(group):
            at = g * group + b
            cols = pl.ds(pl.multiple_of(at * size, size), size)
            scaled = sums[b * rows:(b + 1) * rows] * coef[1:2, cols]
            gathered[me, at] = scaled.astype(jnp.bfloat16)
        for j, peer in enumerate(peers):
            send(me, g, peer, far_send.at[j, g]).start()
        send(me, g, sibling, near_send.at[g]).start()

    part, _, links = chaos_values.shape
    total_rows = modes * rows
    per_row = links * part // total_rows
    column_of = lax.broadcasted_iota(jnp.int32, (1, total_rows), 1) // part
    for n in range(links):
        hits[n:n + 1, :] = (column_of == chaos_index[1, n]).astype(jnp.float32)
    lane_of = lax.broadcasted_iota(jnp.int32, (part, total_rows), 1)
    step_of = lax.broadcasted_iota(jnp.int32, (part, total_rows), 0)
    repeat = (lax.rem(lane_of, part) == step_of).astype(jnp.float32).astype(jnp.bfloat16)
    row_of = lax.broadcasted_iota(jnp.int32, (rows, links), 0)
    owner_of = lax.broadcasted_iota(jnp.int32, (rows, links), 1) // per_row
    owned = owner_of == row_of // part + me * (rows // part)
    built = jnp.zeros((rows, total_rows), jnp.float32)
    for i in range(part):
        spread_out = lax.dot_general(
            chaos_values[i], repeat, (((0,), (0,)), ((), ())), preferred_element_type=jnp.float32)
        placed = (spread_out * hits[0:links, :]).astype(jnp.bfloat16)
        mine = jnp.logical_and(owned, lax.rem(row_of, part) == i).astype(jnp.float32).astype(jnp.bfloat16)
        built = built + jnp.dot(mine, placed, preferred_element_type=jnp.float32)
    matrix[...] = built.astype(jnp.bfloat16)

    weight_copy(0).wait()

    @pl.loop(0, groups)
    def _(t):
        g = turn(t)
        right_copy(g).wait()
        sums = stencil(g, 0)
        for b in range(group):
            at = g * group + b
            cols = pl.ds(pl.multiple_of(at * size, size), size)
            rbuf[:, cols] = rbuf[:, cols] - sums[b * rows:(b + 1) * rows] * coef[0:1, cols]

    def mix(g):
        send(sibling, g, sibling, near_send.at[g]).wait_recv()
        for j, peer in enumerate(peers):
            other = peer + 1 - 2 * lax.rem(peer, 2)
            send(other, g, sibling, forward_send.at[j, g]).wait_recv()
        for b in range(group):
            at = g * group + b
            cols = pl.ds(pl.multiple_of(at * size, size), size)
            mixed = jnp.dot(
                matrix[...], gathered[:, at].reshape(modes * rows, size), preferred_element_type=jnp.float32)
            rbuf[:, cols] = rbuf[:, cols] - mixed

    def forward(g):
        for j, peer in enumerate(peers):
            send(peer, g, peer, far_send.at[j, g]).wait_recv()
            send(peer, g, sibling, forward_send.at[j, g]).start()

    forward(turn(0))

    @pl.loop(1, groups)
    def _(t):
        forward(turn(t))
        mix(turn(t - 1))

    mix(turn(groups - 1))

    @pl.loop(0, groups)
    def _(g):
        send(me, g, sibling, near_send.at[g]).wait_send()
        for j, peer in enumerate(peers):
            send(me, g, peer, far_send.at[j, g]).wait_send()
            send(peer, g, sibling, forward_send.at[j, g]).wait_send()

    @pl.when(has_left)
    def _():
        to_left.wait_send()

    @pl.when(has_right)
    def _():
        to_right.wait_send()


def masked_stencil(low, base, couplings, at, group, weights, taps, size):
    rows = low.shape[1]
    tall = []
    for b in range(group):
        wide = []
        for c in range(taps):
            keep = jnp.full((rows, size), couplings[c, at + b].astype(jnp.float32)).astype(jnp.bfloat16)
            wide.append(low[base + b + c] * keep)
        tall.append(jnp.concatenate(wide, axis=1))
    stacked = jnp.concatenate(tall, axis=0)
    return jnp.dot(stacked, weights.reshape(taps * size, size), preferred_element_type=jnp.float32)


def cheapest_cover(held, adjacent):
    chosen = lax.broadcasted_iota(jnp.int32, (8, 128), 0) * 128 + lax.broadcasted_iota(jnp.int32, (8, 128), 1)
    rest = chosen ^ (2 ** held - 1)
    columns = sum((chosen >> i) & 1 for i in range(held))
    uncovered = sum(jnp.where((rest & links) != 0, 1, 0) for links in adjacent)
    key = ((columns + uncovered) << (held + 4)) + (uncovered << held) + chosen
    key = jnp.where(chosen < 2 ** held, key.astype(jnp.float32), float(2 ** 23))
    return jnp.min(key).astype(jnp.int32)


def slots_of(held, chosen, adjacent):
    used = jnp.int32(0)
    columns = []
    for c in range(held):
        taken = (chosen >> c) & 1
        columns.append(jnp.where(taken == 1, used, -1))
        used = used + taken
    rows = []
    for links in adjacent:
        taken = jnp.where((links & ~chosen) != 0, 1, 0)
        rows.append(jnp.where(taken == 1, used, -1))
        used = used + taken
    return columns, rows


def along(shape, axis, shift, values):
    block = lax.broadcasted_iota(jnp.int32, shape, axis) >> shift
    found = jnp.full(shape, -1, jnp.int32)
    for i, value in enumerate(values):
        found = jnp.where(block == i, value, found)
    return found


def choose_kernel(
    group, fewest,
    field, coefficient, precond, blocks, couplings, chaos_values, chaos_index, index_row,
    choice, slots, kept_links, weights, first, coef, scale, placed,
    values, wide_index, links_smem, sems,
):
    size = blocks.shape[-1]
    part, _, entries = chaos_values.shape
    total = placed.shape[1]
    held = total // part // 2
    shift = held.bit_length() - 1
    per_row = entries // (2 * held)
    near_span = pl.ds((group - REACH) * size, (group + 2 * REACH) * size)
    index_copy = pltpu.make_async_copy(chaos_index, links_smem, sems.at[0])
    row_copy = pltpu.make_async_copy(index_row, wide_index, sems.at[1])
    values_copy = pltpu.make_async_copy(chaos_values, values, sems.at[2])
    coef_copy = pltpu.make_async_copy(coefficient, coef, sems.at[3])
    scale_copy = pltpu.make_async_copy(precond, scale, sems.at[4])
    kept_copy = pltpu.make_async_copy(couplings, kept_links, sems.at[7])
    index_copy.start()
    row_copy.start()
    values_copy.start()
    kept_copy.start()
    tiles = first.shape[0] // 8
    for i in range(tiles):
        pltpu.make_async_copy(
            field.at[pl.ds(i * 8, 8), near_span], first.at[pl.ds(i * 8, 8)], sems.at[5]).start()
    for i in range(weights.shape[0]):
        pltpu.make_async_copy(blocks.at[1, i], weights.at[i], sems.at[6]).start()
    coef_copy.start()
    scale_copy.start()

    index_copy.wait()
    row_copy.wait()
    values_copy.wait()
    adjacent = [[], []]
    for row in range(2 * held):
        side = row // held
        links = jnp.int32(0)
        for n in range(row * per_row, row * per_row + per_row):
            column = links_smem[1, n]
            links = links | (((column >> shift) ^ side) << (column & (held - 1)))
        adjacent[side].append(links)
    best = [cheapest_cover(held, links) for links in adjacent]
    inward = best[0] >> (held + 4)
    needed = jnp.maximum(jnp.maximum(inward, best[1] >> (held + 4)), fewest)
    choice[0, 0] = 2 * (needed - fewest) + jnp.where(inward < needed, 1, 0)
    for side in range(2):
        columns, rows = slots_of(held, best[side] & (2 ** held - 1), adjacent[side])
        for i, value in enumerate(columns + rows):
            slots[0, side * 2 * held + i] = value

    square = (entries, entries)
    wide_row = jnp.broadcast_to(wide_index[1:2, :], square).astype(jnp.float32)
    eye = lax.broadcasted_iota(jnp.int32, square, 0) == lax.broadcasted_iota(jnp.int32, square, 1)
    column_of = jnp.sum(jnp.where(eye, wide_row, 0.0), axis=1, keepdims=True)
    step = part.bit_length() - 1
    lane_block = (lax.broadcasted_iota(jnp.int32, (entries, total), 1) >> step).astype(jnp.float32)
    hits = (lane_block == column_of).astype(jnp.float32)
    lane_of = lax.broadcasted_iota(jnp.int32, (part, total), 1)
    step_of = lax.broadcasted_iota(jnp.int32, (part, total), 0)
    repeat = ((lane_of & (part - 1)) == step_of).astype(jnp.float32).astype(jnp.bfloat16)
    for i in range(part):
        spread_out = lax.dot_general(
            values[i], repeat, (((0,), (0,)), ((), ())), preferred_element_type=jnp.float32)
        placed[i * entries:(i + 1) * entries] = (spread_out * hits).astype(jnp.bfloat16)

    pltpu.make_async_copy(field.at[:, near_span], first, sems.at[5]).wait()
    pltpu.make_async_copy(blocks.at[1], weights, sems.at[6]).wait()
    coef_copy.wait()
    scale_copy.wait()
    kept_copy.wait()


def packed_kernel(
    modes, slabs, group, entries, packed, lean,
    field, right, blocks, slot_of, links, early, first, coef, scale, placed,
    fbuf, rbuf,
    low, later, gathered, outgoing, arrived, picks, matrix,
    load_sem, field_sem, halo_send, halo_recv,
    near_send, near_recv, far_send, far_recv, forward_send, forward_recv,
):
    rows, width = field.shape
    size = blocks.shape[-1]
    count = width // size
    groups = count // group
    span = group * size
    taps = 2 * REACH + 1
    pairs = modes // 2
    both = 2 * rows
    total = 2 * both
    part = picks.shape[0] // packed
    held = both // part
    shift = part.bit_length() - 1
    per_row = entries // (2 * held)
    tall = packed * part
    small = tall - part if lean else tall
    me = lax.axis_index("mode")
    slab = lax.axis_index("mesh")
    sibling = me + 1 - 2 * lax.rem(me, 2)
    peer = lax.rem(me + 2, modes)
    core = lax.rem(me, 2)
    here = me // 2
    share = group // 2
    batch = groups // 4
    has_left = slab > 0
    has_right = slab < slabs - 1

    barrier = pltpu.get_barrier_semaphore()
    for other in [sibling, peer]:
        pl.semaphore_signal(barrier, inc=1, device_id={"mode": other}, device_id_type=MESH)

    @pl.when(has_left)
    def _():
        pl.semaphore_signal(barrier, inc=1, device_id={"mesh": slab - 1}, device_id_type=MESH)

    @pl.when(has_right)
    def _():
        pl.semaphore_signal(barrier, inc=1, device_id={"mesh": slab + 1}, device_id_type=MESH)

    def field_copy(q):
        cols = pl.ds(pl.multiple_of(q * batch * span, span), batch * span)
        return pltpu.make_async_copy(field.at[:, cols], fbuf.at[:, cols], field_sem.at[q])

    later_copy = pltpu.make_async_copy(blocks.at[0], later, load_sem.at[0])
    right_copy = pltpu.make_async_copy(right, rbuf, load_sem.at[1])
    for q in (0, 3, 1, 2):
        field_copy(q).start()
    later_copy.start()
    right_copy.start()

    def lower_block(at):
        cols = pl.ds(pl.multiple_of(at * size, size), size)
        low[REACH + at] = fbuf[:, cols].astype(jnp.bfloat16)

    def lower(g):
        for b in range(group):
            lower_block(g * group + b)

    def near(g):
        ours = gathered.at[core, pl.ds(g * group, group)]
        return pltpu.make_async_remote_copy(
            src_ref=ours, dst_ref=ours, send_sem=near_send, recv_sem=near_recv.at[g & 3],
            device_id={"mode": sibling}, device_id_type=MESH)

    def far(g, height, part_in=None):
        start, length, slot = (0, share, g) if part_in is None else (part_in, 1, part_in * groups)
        return pltpu.make_async_remote_copy(
            src_ref=outgoing.at[pl.ds(g * share + start, length), pl.ds(0, height)],
            dst_ref=arrived.at[pl.ds(g * group + core * share + start, length), pl.ds(0, height)],
            send_sem=far_send, recv_sem=far_recv.at[slot],
            device_id={"mode": peer}, device_id_type=MESH)

    def relay(g, height, part_in=None):
        start, length, slot = (0, share, g) if part_in is None else (part_in, 1, part_in * groups)
        ours = arrived.at[pl.ds(g * group + core * share + start, length), pl.ds(0, height)]
        return pltpu.make_async_remote_copy(
            src_ref=ours, dst_ref=ours, send_sem=forward_send, recv_sem=forward_recv.at[slot],
            device_id={"mode": sibling}, device_id_type=MESH)

    def sized(lean_side, act):
        if not lean:
            act(tall)
            return

        @pl.when(here == lean_side)
        def _():
            act(small)

        @pl.when(here != lean_side)
        def _():
            act(tall)

    def pack(g):
        near(g).wait_recv()
        for b in range(share):
            at = g * group + core * share + b
            outgoing[g * share + b] = jnp.dot(
                picks[...], gathered[:, at].reshape(both, size),
                preferred_element_type=jnp.float32).astype(jnp.bfloat16)

        @pl.when(g != 0)
        def _():
            sized(1, lambda height: far(g, height).start())

        @pl.when(g == 0)
        def _():
            for part_in in range(share):
                sized(1, lambda height: far(0, height, part_in).start())

    def turn(t):
        return lax.rem(t + 1, groups)

    def stencil(g, weights):
        return masked_stencil(low, g * group, links, g * group, group, weights[...], taps, size)

    def spread(g):
        sums = stencil(g, early)
        for b in range(group):
            at = g * group + b
            cols = pl.ds(pl.multiple_of(at * size, size), size)
            scaled = sums[b * rows:(b + 1) * rows] * coef[1:2, cols]
            gathered[core, at] = scaled.astype(jnp.bfloat16)

    for b in range(group + 2 * REACH):
        low[group + b] = first[:, b * size:(b + 1) * size].astype(jnp.bfloat16)

    to_left = pltpu.make_async_remote_copy(
        src_ref=low.at[pl.ds(REACH, REACH)], dst_ref=low.at[pl.ds(REACH + count, REACH)],
        send_sem=halo_send.at[0], recv_sem=halo_recv.at[0],
        device_id={"mesh": slab - 1}, device_id_type=MESH)
    to_right = pltpu.make_async_remote_copy(
        src_ref=low.at[pl.ds(count, REACH)], dst_ref=low.at[pl.ds(0, REACH)],
        send_sem=halo_send.at[1], recv_sem=halo_recv.at[1],
        device_id={"mesh": slab + 1}, device_id_type=MESH)

    lane = lax.broadcasted_iota(jnp.int32, (1, part * entries), 1)
    lane_step = lax.div(lane, entries)
    lane_key = lane_step * 2 * held + lax.div(lane - lane_step * entries, per_row)

    def matrix_rows(height, start):
        row = lax.broadcasted_iota(jnp.int32, (height, 1), 0)
        row_key = (row & (part - 1)) * 2 * held + (row >> shift) + start
        wanted = (row_key == lane_key).astype(jnp.float32).astype(jnp.bfloat16)
        return jnp.dot(wanted, placed[...], preferred_element_type=jnp.float32)

    def half(values, side):
        return jnp.where(side == 0, values[:, 0:both], values[:, both:total])

    def slots_to(side, kind):
        first_slot = [slot_of[0, kind * held + i] for i in range(held)]
        other_slot = [slot_of[0, (2 + kind) * held + i] for i in range(held)]
        return [jnp.where(side == 0, a, b) for a, b in zip(first_slot, other_slot)]

    def chosen_rows(height, values):
        row = lax.broadcasted_iota(jnp.int32, (height, both), 0)
        column = lax.broadcasted_iota(jnp.int32, (height, both), 1)
        same = (row & (part - 1)) == (column & (part - 1))
        slot = along((1, both), 1, shift, values)
        return slot, jnp.logical_and((row >> shift) == slot, same).astype(jnp.float32)

    @pl.loop(0, groups + 1)
    def _(t):
        g = turn(t)

        @pl.when(t == 1)
        def _():
            field_copy(0).wait()
            for at in range(group + group + REACH, 4 * group):
                lower_block(at)

        @pl.when(jnp.logical_and(t >= 2, t + 2 <= groups - 2))
        def _():
            lower(t + 2)

        @pl.when(jnp.logical_and(t == groups - 2, has_right))
        def _():
            to_left.wait_recv()

        @pl.when(jnp.logical_and(t == groups - 1, has_left))
        def _():
            to_right.wait_recv()

        @pl.when(t < groups)
        def _():
            spread(g)

            @pl.when(t == 0)
            def _():
                pl.semaphore_wait(barrier, pairs + jnp.minimum(slab, 1) + jnp.minimum(slabs - 1 - slab, 1))

            near(g).start()

        @pl.when(t == 0)
        def _():
            column_slot, taken = chosen_rows(tall, slots_to(1 - here, 0))
            _, summed = chosen_rows(tall, slots_to(1 - here, 1))
            outward = half(matrix_rows(both, (1 - here) * held), here)
            outward = jnp.where(column_slot < 0, outward, 0.0).astype(jnp.bfloat16)
            picks[...] = (taken + jnp.dot(
                summed.astype(jnp.bfloat16), outward, preferred_element_type=jnp.float32)).astype(jnp.bfloat16)

        @pl.when(t != 1)
        def _():
            pack(turn(jnp.maximum(t - 1, 0)))

        @pl.when(t == 1)
        def _():
            lower_block(0)
            field_copy(3).wait()
            lower(groups - 1)

            @pl.when(has_left)
            def _():
                to_left.start()

            @pl.when(has_right)
            def _():
                to_right.start()

            @pl.when(jnp.logical_not(has_left))
            def _():
                low[pl.ds(0, REACH)] = jnp.zeros((REACH, rows, size), jnp.bfloat16)

            @pl.when(jnp.logical_not(has_right))
            def _():
                low[pl.ds(REACH + count, REACH)] = jnp.zeros((REACH, rows, size), jnp.bfloat16)

            field_copy(1).wait()
            field_copy(2).wait()


    later_copy.wait()
    mine = matrix_rows(rows, me * (held // 2))
    _, arriving = chosen_rows(tall, slots_to(here, 0))
    inward = lax.dot_general(
        half(mine, 1 - here).astype(jnp.bfloat16), arriving.astype(jnp.bfloat16), (((1,), (1,)), ((), ())),
        preferred_element_type=jnp.float32)
    in_rows = slots_to(here, 1)
    my_slots = [jnp.where(core == 0, in_rows[i], in_rows[i + held // 2]) for i in range(held // 2)]
    row = lax.broadcasted_iota(jnp.int32, (rows, tall), 0)
    column = lax.broadcasted_iota(jnp.int32, (rows, tall), 1)
    own = jnp.logical_and(
        (column >> shift) == along((rows, 1), 0, shift, my_slots), (row & (part - 1)) == (column & (part - 1)))
    matrix[:, 0:both] = half(mine, here).astype(jnp.bfloat16)
    matrix[:, both:both + tall] = (inward + own.astype(jnp.float32)).astype(jnp.bfloat16)

    if lean:
        @pl.when(here == 0)
        def _():
            @pl.loop(0, count)
            def _(at):
                arrived[at, small:tall] = jnp.zeros((part, size), jnp.bfloat16)

    def forward(g):
        def act(height):
            far(g, height).wait_recv()
            relay(g, height).start()

        sized(0, act)

    right_copy.wait()
    ahead = groups // 2

    wide = 2 * group

    @pl.loop(0, groups // 2)
    def _(t):
        forward(turn(t))
        base = t * wide
        sums = masked_stencil(low, base, links, base, wide, later[...], taps, size)
        for b in range(wide):
            cols = pl.ds(pl.multiple_of((base + b) * size, size), size)
            rbuf[:, cols] = rbuf[:, cols] - sums[b * rows:(b + 1) * rows] * coef[0:1, cols]

    def mix(at):
        cols = pl.ds(pl.multiple_of(at * size, size), size)
        stacked = jnp.concatenate([gathered[:, at].reshape(both, size), arrived[at]], axis=0)
        mixed = jnp.dot(matrix[...], stacked, preferred_element_type=jnp.float32)
        left = rbuf[:, cols] - mixed
        rbuf[:, cols] = left
        fbuf[:, cols] = fbuf[:, cols] + scale[:, cols] * left

    def forward_part(part_in):
        def act(height):
            far(0, height, part_in).wait_recv()
            relay(0, height, part_in).start()

        sized(0, act)

    @pl.loop(1, groups)
    def _(g):
        @pl.when(jnp.logical_and(g >= ahead, g < groups - 1))
        def _():
            forward(g + 1)

        @pl.when(g == groups - 1)
        def _():
            forward_part(0)

        sized(0, lambda height: relay(g, height).wait_recv())
        for b in range(group):
            mix(g * group + b)

    forward_part(1)
    for part_in in range(share):
        sized(0, lambda height: relay(0, height, part_in).wait_recv())
        mix(part_in)
        mix(share + part_in)

    def drain(source, sem, other):
        pltpu.make_async_remote_copy(
            src_ref=source, dst_ref=source, send_sem=sem, recv_sem=far_recv.at[0],
            device_id={"mode": other}, device_id_type=MESH).wait_send()

    drain(gathered.at[core], near_send, sibling)
    sized(1, lambda height: drain(outgoing.at[:, pl.ds(0, height)], far_send, peer))
    sized(0, lambda height: drain(outgoing.at[:, pl.ds(0, height)], forward_send, sibling))

    @pl.when(has_left)
    def _():
        to_left.wait_send()

    @pl.when(has_right)
    def _():
        to_right.wait_send()


def write_kernel(pieces, kept, found, updated, residual, sems):
    span = kept.shape[1] // pieces

    @pl.loop(0, pieces)
    def _(i):
        some = pl.ds(pl.multiple_of(i * span, span), span)
        pltpu.make_async_copy(found.at[:, some], residual.at[:, some], sems.at[0]).start()
        pltpu.make_async_copy(kept.at[:, some], updated.at[:, some], sems.at[1]).start()

    pltpu.make_async_copy(found, residual, sems.at[0]).wait()
    pltpu.make_async_copy(kept, updated, sems.at[1]).wait()


def finish_kernel(pieces, field, found, precond, updated, residual, stage, sems):
    rows, width = field.shape
    span = width // pieces

    def columns(i):
        return pl.ds(pl.multiple_of(i * span, span), span)

    def found_copy(i):
        return pltpu.make_async_copy(found.at[:, columns(i)], residual.at[:, columns(i)], sems.at[0, i])

    def stage_copy(i):
        return pltpu.make_async_copy(stage.at[:, columns(i)], updated.at[:, columns(i)], sems.at[1, i])

    @pl.loop(0, pieces)
    def _(i):
        found_copy(i).start()
        cols = columns(i)
        stage[:, cols] = field[:, cols] + precond[:, cols] * found[:, cols]
        stage_copy(i).start()

    @pl.loop(0, pieces)
    def _(i):
        found_copy(i).wait()
        stage_copy(i).wait()


def shards(modes, slabs, field, right_side, coefficient, precond, blocks, couplings, chaos_values, chaos_index):
    rows, width = field.shape
    size = blocks.shape[-1]
    taps = blocks.shape[1]
    count = width // size
    group = 4
    groups = count // group
    others = max(modes // 2 - 1, 1)
    inside = pl.BlockSpec(memory_space=pltpu.VMEM)
    anywhere = pl.BlockSpec(memory_space=pl.ANY)
    spare = 67043328 - 2 * rows * width * 4 - 96 * 1024
    scalars = pl.BlockSpec(memory_space=pltpu.SMEM)
    dma = pltpu.SemaphoreType.DMA
    part = chaos_values.shape[1]
    both = 2 * rows
    entries = chaos_values.shape[0]
    common = [
        pltpu.VMEM((count + 2 * REACH, rows, size), jnp.bfloat16),
        pltpu.VMEM(blocks.shape, jnp.bfloat16),
        pltpu.VMEM(coefficient.shape, jnp.float32),
    ]
    waits = [dma((groups,)), dma((groups,)), dma((2,)), dma, dma((2,)), dma((2,))]
    arrays = [pltpu.VMEM((rows, width), jnp.float32)] * 2
    results = [jax.ShapeDtypeStruct((rows, width), jnp.float32)] * 2
    weights_row = precond[None, :]
    links = chaos_index.T
    values = chaos_values.transpose(1, 2, 0)

    def whole():
        kept, found = pl.pallas_call(
            functools.partial(kernel, modes, slabs, group),
            out_shape=arrays,
            in_specs=[anywhere, anywhere, anywhere, anywhere, scalars, inside, scalars],
            out_specs=[inside] * 2,
            scratch_shapes=common + [
                pltpu.VMEM((modes, count, rows, size), jnp.bfloat16),
                pltpu.VMEM((rows, modes * rows), jnp.bfloat16),
                pltpu.VMEM((max(entries, rows), modes * rows), jnp.float32),
            ] + waits + [dma((groups,)), dma((others, groups)), dma((others, groups)), dma((modes, groups))],
            compiler_params=pltpu.CompilerParams(
                collective_id=0, has_side_effects=True, vmem_limit_bytes=spare),
            name="gather_mix",
        )(field, right_side, coefficient, blocks, couplings.T, values, links)
        pieces = 16
        return tuple(pl.pallas_call(
            functools.partial(finish_kernel, pieces),
            out_shape=results,
            in_specs=[inside] * 3,
            out_specs=[anywhere] * 2,
            scratch_shapes=[pltpu.VMEM((rows, width), jnp.float32), dma((2, pieces))],
            compiler_params=pltpu.CompilerParams(vmem_limit_bytes=8 * 1024 * 1024),
            name="finish",
        )(kept, found, weights_row))

    held = both // part
    if modes != 4 or both % part or held != 8 or part & (part - 1) or groups % 4 or groups < 8:
        return whole()
    fewest = held // 2
    near_blocks = group + 2 * REACH

    prepared = pl.pallas_call(
        functools.partial(choose_kernel, group, fewest),
        out_shape=[
            pltpu.SMEM((1, 1), jnp.int32),
            pltpu.SMEM((1, 4 * held), jnp.int32),
            pltpu.SMEM((taps, count), jnp.int32),
            pltpu.VMEM(blocks.shape[1:], jnp.bfloat16),
            pltpu.VMEM((rows, near_blocks * size), jnp.float32),
            pltpu.VMEM(coefficient.shape, jnp.float32),
            pltpu.VMEM((1, width), jnp.float32),
            pltpu.VMEM((part * entries, 2 * both), jnp.bfloat16),
        ],
        in_specs=[anywhere] * 8,
        out_specs=[scalars] * 3 + [inside] * 5,
        scratch_shapes=[
            pltpu.VMEM(values.shape, jnp.bfloat16),
            pltpu.VMEM(links.shape, jnp.int32),
            pltpu.SMEM(links.shape, jnp.int32),
            dma((8,)),
        ],
        compiler_params=pltpu.CompilerParams(vmem_limit_bytes=67043328 - 5 * 512 * 1024),
        name="choose",
    )(field, coefficient, weights_row, blocks, couplings.T, values, links, links)

    def reduced(packed, lean, *operands):
        tall = packed * part
        kept, found = pl.pallas_call(
            functools.partial(packed_kernel, modes, slabs, group, entries, packed, lean),
            out_shape=arrays,
            in_specs=[anywhere] * 3 + [scalars] * 2 + [inside] * 5,
            out_specs=[inside] * 2,
            scratch_shapes=[
                pltpu.VMEM((count + 2 * REACH, rows, size), jnp.bfloat16),
                pltpu.VMEM(blocks.shape[1:], jnp.bfloat16),
                pltpu.VMEM((2, count, rows, size), jnp.bfloat16),
                pltpu.VMEM((count // 2, tall, size), jnp.bfloat16),
                pltpu.VMEM((count, tall, size), jnp.bfloat16),
                pltpu.VMEM((tall, both), jnp.bfloat16),
                pltpu.VMEM((rows, both + tall), jnp.bfloat16),
                dma((2,)), dma((4,)), dma((2,)), dma((2,)),
                dma, dma((4,)), dma, dma((groups + 1,)), dma, dma((groups + 1,)),
            ],
            compiler_params=pltpu.CompilerParams(
                collective_id=2 * packed + lean, has_side_effects=True, vmem_limit_bytes=spare - 4 * 1024 * 1024),
            name="gather_mix",
        )(*operands)
        return tuple(pl.pallas_call(
            functools.partial(write_kernel, count),
            out_shape=results,
            in_specs=[inside] * 2,
            out_specs=[anywhere] * 2,
            scratch_shapes=[dma((2,))],
            compiler_params=pltpu.CompilerParams(vmem_limit_bytes=8 * 1024 * 1024),
            name="write",
        )(kept, found))

    return _switch_internal(
        prepared[0][0, 0],
        [functools.partial(reduced, packed, lean) for packed in range(fewest, held + 1) for lean in (False, True)],
        (field, right_side, blocks, *prepared[1:]), branches_platforms=None)


def solution(mesh):
    placed = (
        P("mode", "mesh"),
        P("mode", "mesh"),
        P(None, "mesh"),
        P("mesh"),
        P(),
        P("mesh", None),
        P(),
        P(),
    )
    return jax.shard_map(
        functools.partial(shards, mesh.shape["mode"], mesh.shape["mesh"]),
        mesh=mesh,
        in_specs=placed,
        out_specs=(P("mode", "mesh"), P("mode", "mesh")),
        check_vma=False,
    )
```
